128 devices in a mesh: row: 4 (over y), col: 32 (over x, z, core).
Axes of the slice: x: 4, y: 4, z: 4, core: 2. Of those that a mesh axis runs over, the one named last changes fastest.
Arguments:
- vectors: float32 [16, 1048576], P(None, ('row', 'col')), may hold values from -6 to 6
- coords: float32 [3, 1048576], P(None, ('row', 'col')), may hold values from 0 to 1
- leaf_basis: bfloat16 [4096, 64, 256], P(('row', 'col')), may hold values from -0.375 to 0.375
- transfer: bfloat16 [8192, 4096], P(('row', 'col')), may hold values from -0.5 to 0.5
- coupling: bfloat16 [8192, 6, 4096], P(('row', 'col')), may hold values from -0.3125 to 0.3125
- near_list: int32 [4096, 8], P(('row', 'col')), may hold values from 0 to 4095, as said below
- near_count: int32 [4096], P(('row', 'col')), may hold values from 1 to 8, as said below
- local_list: int32 [8192, 6], P(('row', 'col')), may hold values from 1 to 8191, as said below
- top_transfer: bfloat16 [256, 4096], replicated, may hold values from -0.5 to 0.5
- top_coupling: bfloat16 [256, 2, 4096], replicated, may hold values from -0.5 to 0.5
- top_list: int32 [256, 2], replicated, may hold values from 1 to 255, as said below
Outputs:
- product: float32 [16, 1048576], P(None, ('row', 'col'))
The draws below stay inside these ranges and needn't reach their ends.
Inputs may be any that keep to these rules, and one draw needn't show every extreme that they name: `near_list`: entry 0 of a leaf's list is the leaf itself; every entry names a leaf of the same device or of the device just before or after it in the order of row then col; entries past near_count are ignored. `near_count`: devices differ in how full their leaves' lists are. `local_list`: a slot's partners are slots of the same level of the subtrees of the same device or of the device just before or after it; the rows of slots 0 and 1 are ignored. `top_list`: a slot's partners are upper slots of the same level; rows 0 and 1 are ignored.
All inputs are finite; a program needn't handle non-finite values.
Results may differ from the reference program's by a relative error of at most 0.0003.
Values sent between devices are 32-bit elements; how exact they have to be, the bound alone decides.
No kernel may reach another device: no remote copies, remote signals or barrier semaphores. Data moves between devices by JAX's collectives and lax.ppermute only.
A program may use at most 128 MiB of HBM per device.

```python
import math
import jax
import jax.numpy as jnp
from jax import lax

LEAF = 256
RANK = 64
VECS = 16
LEAF_DEV = 32
NEAR = 8
FAR = 6
TOP_FAR = 2
DEVS = 128
LEAVES = 4096
POINTS = 1048576
SLOTS = 8192
TOP_SLOTS = 256
N_ROW = 4
N_COL = 32


def level_base(slot_ids, limit):
    safe = jnp.maximum(slot_ids, 1)
    level = jnp.zeros_like(safe)
    power = 1
    while power <= limit:
        level = level + (safe >= power).astype(jnp.int32)
        power = power * 2
    return jnp.power(2, level - 1).astype(jnp.int32)


def draw_near_list(key, part):
    leaf_ids = jnp.arange(LEAVES, dtype=jnp.int32)
    owner = leaf_ids // LEAF_DEV
    first_key, second_key = jax.random.split(jax.random.fold_in(key, 11))
    steps = jax.random.randint(first_key, (LEAVES, NEAR), -1, 2)
    partner_dev = jnp.clip(owner[:, None] + steps, 0, DEVS - 1)
    picks = jax.random.randint(second_key, (LEAVES, NEAR), 0, LEAF_DEV)
    chosen = partner_dev * LEAF_DEV + picks
    chosen = chosen.at[:, 0].set(leaf_ids)
    return chosen.astype(jnp.int32)


def draw_near_count(key, part):
    leaf_ids = jnp.arange(LEAVES, dtype=jnp.int32)
    owner = leaf_ids // LEAF_DEV
    first_key, second_key = jax.random.split(jax.random.fold_in(key, 23))
    ceiling = jax.random.randint(first_key, (DEVS,), 1, NEAR + 1)
    ceiling = ceiling.at[0].set(NEAR)
    spread = jax.random.randint(second_key, (LEAVES,), 0, NEAR)
    counts = 1 + spread % ceiling[owner]
    counts = counts.at[0].set(NEAR).at[1].set(1)
    return counts.astype(jnp.int32)


def draw_local_list(key, part):
    subtree = 2 * LEAF_DEV
    global_ids = jnp.arange(SLOTS, dtype=jnp.int32)
    owner = global_ids // subtree
    slot_ids = global_ids % subtree
    base = level_base(slot_ids, subtree)
    first_key, second_key = jax.random.split(jax.random.fold_in(key, 37))
    steps = jax.random.randint(first_key, (SLOTS, FAR), -1, 2)
    partner_dev = jnp.clip(owner[:, None] + steps, 0, DEVS - 1)
    picks = jax.random.randint(second_key, (SLOTS, FAR), 0, subtree) % base[:, None]
    chosen = partner_dev * subtree + base[:, None] + picks
    chosen = chosen.at[0, 0].set(1).at[SLOTS - 1, 0].set(SLOTS - 1)
    return chosen.astype(jnp.int32)


def draw_top_list(key, part):
    slot_ids = jnp.arange(TOP_SLOTS, dtype=jnp.int32)
    base = level_base(slot_ids, TOP_SLOTS)
    picks = jax.random.randint(jax.random.fold_in(key, 41), (TOP_SLOTS, TOP_FAR), 0, TOP_SLOTS) % base[:, None]
    chosen = base[:, None] + picks
    chosen = chosen.at[TOP_SLOTS - 1, 0].set(TOP_SLOTS - 1)
    return chosen.astype(jnp.int32)


def block_scale(rng, dims, cuts, smallest, top_value):
    loudness = 1.0
    for axis_at, parts in cuts:
        steps = jax.random.uniform(jax.random.fold_in(jax.random.fold_in(rng, 6), axis_at), (parts,), jnp.float32, smallest / len(cuts), top_value / len(cuts))
        loudness = loudness * jnp.repeat(jnp.exp(steps), dims[axis_at] // parts).reshape((-1,) + (1,) * (len(dims) - 1 - axis_at))
    return loudness


def scatter_about(rng, extent, scale, bound, shards=(), held_as=jnp.bfloat16):
    array = jax.random.normal(rng, extent, jnp.float32) * scale
    if len(shards) > 0:
        array = block_scale(rng, extent, shards, -0.22, 0.18) * array
    return jnp.clip(array, min=-bound, max=bound).astype(held_as)


def setup_inputs(seed: int = 0) -> dict:
    key_of = jax.random.split(jax.random.key(seed), 12)
    vectors = scatter_about(key_of[0], (VECS, POINTS), 1.0, 6.0, ((1, 128),), jnp.float32)
    coords = jnp.clip(1.0 * jax.random.uniform(key_of[1], (3, POINTS), jnp.float32) ** block_scale(key_of[1], (3, POINTS), ((1, 128),), -0.2, 0.2), 0.0, 1.0)
    leaf_basis = scatter_about(key_of[2], (LEAVES, RANK, LEAF), LEAF ** -0.5, 0.375, ((0, 128),))
    transfer = scatter_about(key_of[3], (SLOTS, RANK * RANK), (2 * RANK) ** -0.5, 0.5, ((0, 128),))
    coupling = scatter_about(key_of[4], (SLOTS, FAR, RANK * RANK), (FAR * RANK) ** -0.5, 0.3125, ((0, 128),))
    near_list = draw_near_list(jax.random.fold_in(key_of[11], 71), 0)
    near_count = draw_near_count(jax.random.fold_in(key_of[11], 71), 0)
    local_list = draw_local_list(jax.random.fold_in(key_of[11], 71), 0)
    top_transfer = scatter_about(key_of[8], (TOP_SLOTS, RANK * RANK), (2 * RANK) ** -0.5, 0.5)
    top_coupling = scatter_about(key_of[9], (TOP_SLOTS, TOP_FAR, RANK * RANK), (TOP_FAR * RANK) ** -0.5, 0.5)
    top_list = draw_top_list(jax.random.fold_in(key_of[11], 71), 0)
    return dict(vectors=vectors, coords=coords, leaf_basis=leaf_basis, transfer=transfer, coupling=coupling, near_list=near_list, near_count=near_count, local_list=local_list, top_transfer=top_transfer, top_coupling=top_coupling, top_list=top_list)


HIGHEST_PREC = lax.Precision.HIGHEST
ROOT_THREE = 1.7320508075688772
LENGTH_SCALE = 0.2
JITTER_SQ = 0.0001

def near_leaf(own_coords, partner_ids, partner_count, table):
    chosen = jnp.take(table, partner_ids, axis=1)
    offsets = own_coords[:, :, None, None] - chosen[:3, None, :, :]
    distance = jnp.sqrt(lax.optimization_barrier(jnp.sum(offsets * offsets, axis=0)) + JITTER_SQ)
    scaled = ROOT_THREE * distance / LENGTH_SCALE
    active = (jnp.arange(partner_ids.shape[0], dtype=jnp.int32) < partner_count).astype(jnp.float32)
    matern = (1.0 + scaled) * jnp.exp(-scaled) * active[None, :, None] / math.sqrt(own_coords.shape[1])
    return jnp.einsum('anb,vnb->va', matern, chosen[3:], precision=HIGHEST_PREC)

def upward_level(skeleton, matrices, half_size):
    children = skeleton[..., 2 * half_size:4 * half_size, :, :]
    blocks = matrices[..., 2 * half_size:4 * half_size, :, :]
    products = jnp.einsum('...svr,...srq->...svq', children, blocks, precision=HIGHEST_PREC)
    new_shape = products.shape[:-3] + (half_size, 2) + products.shape[-2:]
    return products.reshape(new_shape).sum(axis=-3)

def downward_level(field, matrices, half_size):
    parents = field[..., half_size:2 * half_size, :, :]
    doubled = jnp.repeat(parents, 2, axis=-3)
    blocks = matrices[..., 2 * half_size:4 * half_size, :, :]
    added = jnp.einsum('...svq,...srq->...svr', doubled, blocks, precision=HIGHEST_PREC)
    return field.at[..., 2 * half_size:4 * half_size, :, :].add(added)

def reference(vectors, coords, leaf_basis, transfer, coupling, near_list, near_count, local_list, top_transfer, top_coupling, top_list):
    devices = N_ROW * N_COL
    subtree = 2 * LEAF_DEV
    basis = leaf_basis.astype(jnp.float32)
    grouped = vectors.reshape(VECS, LEAVES, LEAF).transpose(1, 0, 2)
    leaf_skel = jnp.einsum('cvl,crl->cvr', grouped, basis, precision=HIGHEST_PREC)
    matrices = transfer.astype(jnp.float32).reshape(devices, subtree, RANK, RANK)
    skeleton = jnp.zeros((devices, subtree, VECS, RANK), jnp.float32)
    skeleton = skeleton.at[:, LEAF_DEV:].set(leaf_skel.reshape(devices, LEAF_DEV, VECS, RANK))
    half_size = LEAF_DEV // 2
    while half_size >= 1:
        skeleton = skeleton.at[:, half_size:2 * half_size].set(upward_level(skeleton, matrices, half_size))
        half_size = half_size // 2
    top_mats = top_transfer.astype(jnp.float32).reshape(2 * devices, RANK, RANK)
    upper = jnp.zeros((2 * devices, VECS, RANK), jnp.float32).at[devices:].set(skeleton[:, 1])
    half_size = devices // 2
    while half_size >= 2:
        upper = upper.at[half_size:2 * half_size].set(upward_level(upper, top_mats, half_size))
        half_size = half_size // 2
    top_blocks = top_coupling.astype(jnp.float32).reshape(2 * devices, TOP_FAR, RANK, RANK)
    upper_field = jnp.einsum('skvr,skrq->svq', upper[top_list], top_blocks, precision=HIGHEST_PREC)
    upper_field = upper_field.at[:2].set(0.0)
    half_size = 2
    while half_size < devices:
        upper_field = downward_level(upper_field, top_mats, half_size)
        half_size = half_size * 2
    flat = skeleton.reshape(devices * subtree, VECS, RANK)

    def couple_device(items):
        lists, blocks = items
        partners = flat[lists]
        mats = blocks.astype(jnp.float32).reshape(subtree, FAR, RANK, RANK)
        return jnp.einsum('skvr,skrq->svq', partners, mats, precision=HIGHEST_PREC)
    field = lax.map(couple_device, (local_list.reshape(devices, subtree, FAR), coupling.reshape(devices, subtree, FAR, RANK * RANK)))
    field = field.at[:, 0].set(0.0)
    field = field.at[:, 1].set(upper_field[devices:])
    half_size = 1
    while half_size < LEAF_DEV:
        field = downward_level(field, matrices, half_size)
        half_size = half_size * 2
    leaf_field = field[:, LEAF_DEV:].reshape(LEAVES, VECS, RANK)
    far_part = jnp.einsum('cvr,crl->cvl', leaf_field, basis, precision=HIGHEST_PREC)
    table = jnp.concatenate([coords, vectors], axis=0).reshape(3 + VECS, LEAVES, LEAF)
    own = coords.reshape(3, LEAVES, LEAF).transpose(1, 0, 2)

    def near_item(items):
        return near_leaf(items[0], items[1], items[2], table)
    near_part = lax.map(near_item, (own, near_list, near_count))
    return (far_part + near_part).transpose(1, 0, 2).reshape(VECS, POINTS)
```

```python
import functools
import math

import jax
import jax.numpy as jnp
from jax import lax
from jax.experimental import pallas as pl
from jax.experimental.pallas import tpu as pltpu
from jax.sharding import PartitionSpec as P

AXES = ("row", "col")
BF = jnp.bfloat16
F32 = jnp.float32
LOG2E = 1.4426950408889634
LN2 = 0.6931471805599453
JITTER_SQ = 0.0001
SIGMA = math.sqrt(3.0) / 0.2 * LOG2E
LEAF, RANK, VECS, LEAF_DEV, NEAR, FAR = 256, 64, 16, 32, 8, 6
ROWS = 32
GROUP = 4
NN = (((1,), (0,)), ((), ()))
NT = (((1,), (1,)), ((), ()))
SMEM = pl.BlockSpec(memory_space=pltpu.SMEM)
VMEM = pl.BlockSpec(memory_space=pltpu.VMEM)
ANY = pl.BlockSpec(memory_space=pl.ANY)


def dot(a, b, dims=NN):
    return lax.dot_general(a, b, dims, preferred_element_type=F32)


def pieces(x):
    hi = x.astype(BF)
    lo = (x - hi.astype(F32)).astype(BF)
    return jnp.concatenate([hi, lo], axis=0)


def folded(y):
    half = y.shape[0] // 2
    return y[:half] + y[half:]


def low_lanes(shape):
    return lax.broadcasted_iota(jnp.int32, shape, 1) < RANK


def joined(a, b):
    return jnp.where(low_lanes(a.shape), a, b)


def swapped(x):
    return pltpu.roll(x, RANK, 1)


def order_matrix(transposed):
    row = lax.broadcasted_iota(jnp.int32, (128, 128), 1 if transposed else 0)
    col = lax.broadcasted_iota(jnp.int32, (128, 128), 0 if transposed else 1)
    at = col % RANK
    source = jnp.where(at < 32, 2 * at, 2 * at - 63) + (col // RANK) * RANK
    return jnp.where(row == source, 1.0, 0.0).astype(BF)


def unpack_rows(load, tiles, block):
    for i in range(ROWS):
        tiles[pl.ds(i * 16, 16), :] = load(i).astype(F32)
    for s in range(16):
        block(s, tiles[pl.ds(s, ROWS, stride=16), :])


def pack_transfer(load, tiles, order, write):
    held = [None] * 16

    def keep(s, x):
        held[s] = x

    unpack_rows(load, tiles, keep)
    for s in range(16):
        x = dot(held[s].astype(BF), order)
        y = swapped(x)
        parent_odd = (s // 2) % 2
        rows = [y, x] if parent_odd else [x, y]
        write(s // 2, s % 2, jnp.concatenate(rows, axis=0).astype(BF))


def up_kernel(vec, basis, transfer, sk, dev, ee, xs, tiles, nat):
    order = order_matrix(False)

    def group(g, _):
        base = pl.multiple_of(g * 16, 16)

        def write(m, child, value):
            ee[g * 8 + m, pl.ds(child * RANK, RANK), :] = value

        pack_transfer(
            lambda i: transfer[pl.ds(base, 16), pl.ds(i * 128, 128)], tiles, order, write
        )
        return 0

    lax.fori_loop(0, 4, group, 0)
    for i in range(LEAF_DEV):
        xs[i] = pieces(vec[:, i * LEAF : (i + 1) * LEAF])
    for m in range(LEAF_DEV // 2):
        x = xs[2 * m : 2 * m + 2].reshape(64, LEAF)
        b = basis[2 * m : 2 * m + 2].reshape(128, LEAF)
        r = dot(x, b, NT)
        nat[m] = joined(folded(r[:32]), folded(r[32:]))
    for m in range(LEAF_DEV // 2):
        sk[16 + m] = folded(dot(pieces(nat[m]), order))
    half = LEAF_DEV // 2
    while half > 1:
        for m in range(half, 2 * half, 2):
            a = folded(dot(pieces(sk[m]), ee[m]))
            b = folded(dot(pieces(sk[m + 1]), ee[m + 1]))
            sk[m // 2] = joined(a, b)
        half = half // 2
    top = folded(dot(pieces(sk[1]), ee[1]))
    sk[0] = jnp.where(low_lanes(top.shape), 0.0, top)
    dev[...] = joined(swapped(top[:8]), top[8:])


def split3(v):
    h1 = v.astype(BF).astype(F32)
    h2 = (v - h1).astype(BF).astype(F32)
    return h1, h2, (v - h1 - h2).astype(BF).astype(F32)


def features(c):
    n = c.shape[1]
    s = (c - 0.5) * SIGMA
    blank = jnp.zeros((5, n), F32)
    one = jnp.ones((3, n), F32)
    two = jnp.zeros((2, n), F32)
    h = split3(s)
    size = jnp.sum(s * s, axis=0, keepdims=True)
    own, partner = [], []
    for i, j in ((0, 0), (0, 1), (1, 0), (1, 1), (0, 2), (2, 0)):
        own += [-2.0 * h[j], blank]
        partner += [h[i], blank]
    own += [*split3(size + JITTER_SQ * SIGMA * SIGMA), one, two, jnp.zeros((8, n), F32)]
    partner += [one, *split3(size), two, jnp.zeros((8, n), F32)]
    return jnp.concatenate(own, axis=0), jnp.concatenate(partner, axis=0)


def near_kernel(
    lists, counts, where, xs_own, wide_own, wide_before, wide_after, out, xs, partner, own, pairs
):
    first = (where[0] - 1) * LEAF_DEV
    out[...] = jnp.zeros_like(out)
    xs[pl.ds(LEAF_DEV, LEAF_DEV)] = xs_own[...]
    xs[3 * LEAF_DEV] = jnp.zeros((32, LEAF), BF)
    for at, wide in enumerate((wide_before, wide_own, wide_after)):

        def prepare(i, _):
            lanes = pl.ds(pl.multiple_of(i * LEAF, LEAF), LEAF)
            if at != 1:
                xs[at * LEAF_DEV + i] = pieces(wide[0:VECS, lanes])
            mine, theirs = features(wide[VECS : VECS + 3, lanes])
            partner[at * LEAF_DEV + i] = theirs.T.astype(BF)
            if at == 1:
                own[i] = mine.astype(BF)
            return 0

        lax.fori_loop(0, LEAF_DEV, prepare, 0)

    partner[3 * LEAF_DEV] = partner[LEAF_DEV]

    def enlist(c, total):
        live = counts[c]
        for m in range(NEAR):
            pairs[total] = (lists[m, c] - first) * LEAF_DEV + c
            total = total + (m < live).astype(jnp.int32)
        return total

    total = lax.fori_loop(0, LEAF_DEV, enlist, 0)
    for g in range(GROUP):
        pairs[total + g] = 3 * LEAF_DEV * LEAF_DEV

    def step(i, _):
        for g in range(GROUP):
            code = pairs[i * GROUP + g]
            p = code // LEAF_DEV
            c = code % LEAF_DEV
            t = dot(partner[p], own[c])
            u = t * lax.rsqrt(t)
            k = (u + LOG2E) * jnp.exp2(-u)
            khi = k.astype(BF)
            klo = (k - khi.astype(F32)).astype(BF)
            x = xs[p]
            r = folded(dot(x, khi)) + dot(x[:VECS], klo)
            lanes = pl.ds(pl.multiple_of(c * LEAF, LEAF), LEAF)
            out[:, lanes] = out[:, lanes] + r
        return 0

    lax.fori_loop(0, (total + GROUP - 1) // GROUP, step, 0)


def top_kernel(
    devices,
    lists,
    places,
    where,
    tiles_in,
    transfer,
    coupling,
    out,
    ee,
    q,
    tiles,
    blocks,
    raw,
    sem,
):
    d = where[0]
    levels = devices.bit_length() - 1
    order = order_matrix(False)
    nodes = [(devices + d) >> (levels - level) for level in range(levels + 1)]
    copies = [
        pltpu.make_async_copy(coupling.at[nodes[level]], raw.at[level], sem.at[level])
        for level in range(1, levels + 1)
    ]
    for c in copies:
        c.start()

    def group(g, _):
        base = pl.multiple_of(g * 16, 16)

        def write(m, child, value):
            ee[g * 8 + m, pl.ds(child * RANK, RANK), :] = value

        pack_transfer(
            lambda i: transfer[pl.ds(base, 16), pl.ds(i * 128, 128)], tiles, order, write
        )
        return 0

    lax.fori_loop(0, 2 * devices // 16, group, 0)

    def place(m, _):
        a = tiles_in[places[(2 * m) ^ d]]
        b = tiles_in[places[(2 * m + 1) ^ d]]
        q[devices // 2 + m, 0:8] = joined(a, swapped(b))
        q[devices // 2 + m, 8:16] = joined(swapped(a), b)
        return 0

    lax.fori_loop(0, devices // 2, place, 0, unroll=4)
    half = devices // 2

    def parents(m):
        a = folded(dot(pieces(q[m]), ee[m]))
        b = folded(dot(pieces(q[m + 1]), ee[m + 1]))
        return joined(a, b)

    while half >= 2:
        if half >= 16:

            def some(i, _, half=half):
                for u in range(4):
                    m = half + 8 * i + 2 * u
                    q[m // 2] = parents(m)
                return 0

            lax.fori_loop(0, half // 8, some, 0)
        else:
            for m in range(half, 2 * half, 2):
                q[m // 2] = parents(m)
        half = half // 2
    for c in copies:
        c.wait()
    own = []
    for level in range(1, levels + 1):
        a = nodes[level]
        x = raw[level].astype(F32)
        for i in range(ROWS):
            blocks[pl.ds(i * 8, 2), :] = x[:, i * 128 : (i + 1) * 128]
        rhs, lhs = [], []
        for k in range(2):
            c = blocks[pl.ds(k, ROWS, stride=8), :]
            rhs += [c, swapped(c)]
            slot = lists[k, a]
            v = q[slot // 2]
            lhs.append(jnp.where(slot % 2 == k, v, swapped(v)))
        r = dot(pieces(joined(*lhs)), jnp.concatenate(rhs, axis=0).astype(BF))
        r = folded(dot(pieces(folded(r)), order))
        odd = a % 2 == 1
        r = jnp.where(odd, swapped(r), r)
        own.append(jnp.where(low_lanes(r.shape) != odd, r, 0.0))
    path = own[0]
    for level in range(2, levels + 1):
        r = folded(dot(pieces(path), ee[nodes[level - 1]], NT))
        odd = nodes[level] % 2 == 1
        path = jnp.where(low_lanes(r.shape) != odd, r, 0.0) + own[level - 1]
    out[...] = jnp.where(nodes[levels] % 2 == 1, path, swapped(path))


def down_kernel(
    lists,
    where,
    sk_own,
    sk_before,
    sk_after,
    coupling,
    ee,
    basis,
    path,
    near,
    out,
    table,
    blocks,
    tiles,
    field,
):
    slots = 2 * LEAF_DEV
    first = (where[0] - 1) * slots
    order = order_matrix(False)
    back = order_matrix(True)
    for at, sk in enumerate((sk_before, sk_own, sk_after)):

        def double(m, _):
            x = sk[m]
            y = swapped(x)
            table[at * slots + 2 * m] = pieces(joined(x, y))
            table[at * slots + 2 * m + 1] = pieces(joined(y, x))
            return 0

        lax.fori_loop(0, LEAF_DEV, double, 0, unroll=4)
    for k in range(FAR):

        def group(g, _):
            base = pl.multiple_of(g * 16, 16)

            def write(s, c):
                y = swapped(c)
                rows = [y, c] if s % 2 else [c, y]
                blocks[g * 16 + s, k * RANK : (k + 1) * RANK, :] = jnp.concatenate(
                    rows, axis=0
                ).astype(BF)

            unpack_rows(
                lambda i: coupling[k, pl.ds(base, 16), pl.ds(i * 128, 128)], tiles, write
            )
            return 0

        lax.fori_loop(0, slots // 16, group, 0)

    def couple(m, _):
        sides = []
        for side in range(2):
            j = 2 * m + side
            parts = []
            for k in range(0, FAR, 2):
                a = table[lists[k, j] - first]
                b = table[lists[k + 1, j] - first]
                parts.append(joined(a, b))
            sides.append(folded(dot(jnp.concatenate(parts, axis=1), blocks[j])))
        field[m] = folded(dot(pieces(joined(*sides)), order))
        return 0

    lax.fori_loop(1, LEAF_DEV, couple, 0)
    field[0] = path[...]
    for m in range(1, LEAF_DEV):
        x = field[m // 2]
        x = jnp.where(low_lanes(x.shape) != (m % 2 == 1), x, 0.0)
        field[m] = field[m] + folded(dot(pieces(x), ee[m], NT))
    for m in range(LEAF_DEV // 2):
        x = folded(dot(pieces(field[LEAF_DEV // 2 + m]), back))
        low = low_lanes(x.shape)
        lhs = jnp.concatenate(
            [pieces(jnp.where(low, x, 0.0)), pieces(jnp.where(low, 0.0, x))], axis=0
        )
        r = dot(lhs, basis[2 * m : 2 * m + 2].reshape(128, LEAF))
        for side in range(2):
            lanes = slice((2 * m + side) * LEAF, (2 * m + side + 1) * LEAF)
            far = folded(r[32 * side : 32 * side + 32])
            out[:, lanes] = far + near[:, lanes] * (LN2 / math.sqrt(LEAF))


def call(kernel, out_shape, in_specs, scratch=(), name=None, cost=None):
    return pl.pallas_call(
        kernel,
        out_shape=out_shape,
        in_specs=in_specs,
        out_specs=jax.tree.map(lambda _: VMEM, out_shape),
        scratch_shapes=list(scratch),
        compiler_params=pltpu.CompilerParams(vmem_limit_bytes=48 << 20),
        name=name,
        cost_estimate=cost,
    )


def shaped(shape, dtype=F32):
    return jax.ShapeDtypeStruct(shape, dtype)


def exchange_bits(devices):
    if devices == 128:
        return [2, 4, 6, 1, 3, 5, 0]
    return list(range(devices.bit_length() - 1))


def gathered(tile, devices):
    for bit in exchange_bits(devices):
        swap = [(i, i ^ (1 << bit)) for i in range(devices)]
        tile = jnp.concatenate([tile, lax.ppermute(tile, AXES, swap)], axis=0)
    return tile


def places_of(devices):
    bits = exchange_bits(devices)
    places = [
        sum(((x >> bit) & 1) << at for at, bit in enumerate(bits)) for x in range(devices)
    ]
    return jnp.array(places, jnp.int32)


def per_device(
    vectors,
    coords,
    leaf_basis,
    transfer,
    coupling,
    near_list,
    near_count,
    local_list,
    top_transfer,
    top_coupling,
    top_list,
):
    devices = lax.axis_size(AXES)
    position = lax.axis_index(AXES).astype(jnp.int32)
    where = position.reshape(1)
    up = [(i, i + 1) for i in range(devices - 1)]
    down = [(j, i) for i, j in up]
    wide = jnp.concatenate([vectors, coords], axis=0)
    wide_before = lax.ppermute(wide, AXES, up)
    wide_after = lax.ppermute(wide, AXES, down)
    sk, dev, ee, xs = call(
        up_kernel,
        (
            shaped((LEAF_DEV, VECS, 128)),
            shaped((8, 128)),
            shaped((LEAF_DEV, 128, 128), BF),
            shaped((LEAF_DEV, 32, LEAF), BF),
        ),
        [VMEM] * 3,
        [pltpu.VMEM((512, 128), F32), pltpu.VMEM((16, VECS, 128), F32)],
        "up",
    )(vectors, leaf_basis, transfer)
    sk_before = lax.ppermute(sk, AXES, up)
    sk_after = lax.ppermute(sk, AXES, down)
    tiles = gathered(dev[None], devices)
    near = call(
        near_kernel,
        shaped((VECS, LEAF_DEV * LEAF)),
        [SMEM] * 3 + [VMEM] * 4,
        [
            pltpu.VMEM((3 * LEAF_DEV + 1, 32, LEAF), BF),
            pltpu.VMEM((3 * LEAF_DEV + 1, LEAF, RANK), BF),
            pltpu.VMEM((LEAF_DEV, RANK, LEAF), BF),
            pltpu.SMEM((LEAF_DEV * NEAR + GROUP,), jnp.int32),
        ],
        "near",
    )(near_list.T, near_count, where, xs, wide, wide_before, wide_after)
    levels = devices.bit_length() - 1
    path = call(
        functools.partial(top_kernel, devices),
        shaped((VECS, 128)),
        [SMEM] * 3 + [VMEM] * 2 + [ANY],
        [
            pltpu.VMEM((devices, 128, 128), BF),
            pltpu.VMEM((devices, VECS, 128), F32),
            pltpu.VMEM((512, 128), F32),
            pltpu.VMEM((256, 128), F32),
            pltpu.VMEM((levels + 1, 2, RANK * RANK), BF),
            pltpu.SemaphoreType.DMA((levels + 1,)),
        ],
        "top",
    )(top_list.T, places_of(devices), where, tiles, top_transfer, top_coupling)
    return call(
        down_kernel,
        shaped((VECS, LEAF_DEV * LEAF)),
        [SMEM] * 2 + [VMEM] * 8,
        [
            pltpu.VMEM((6 * LEAF_DEV, 32, 128), BF),
            pltpu.VMEM((2 * LEAF_DEV, FAR * RANK, 128), BF),
            pltpu.VMEM((512, 128), F32),
            pltpu.VMEM((LEAF_DEV, VECS, 128), F32),
        ],
        "down",
    )(
        local_list.T,
        where,
        sk,
        sk_before,
        sk_after,
        jnp.transpose(coupling, (1, 0, 2)),
        ee,
        leaf_basis,
        path,
        near,
    )


def solution(mesh):
    split = P(None, AXES)
    return jax.shard_map(
        per_device,
        mesh=mesh,
        in_specs=(
            split,
            split,
            P(AXES, None, None),
            P(AXES, None),
            P(AXES, None, None),
            P(AXES, None),
            P(AXES),
            P(AXES, None),
            P(),
            P(),
            P(),
        ),
        out_specs=split,
        check_vma=False,
    )
```

```python
import functools
import math

import jax
import jax.numpy as jnp
from jax import lax
from jax.experimental import pallas as pl
from jax.experimental.pallas import tpu as pltpu
from jax.sharding import PartitionSpec as P

AXES = ("row", "col")
BF = jnp.bfloat16
F32 = jnp.float32
LOG2E = 1.4426950408889634
LN2 = 0.6931471805599453
JITTER_SQ = 0.0001
SIGMA = math.sqrt(3.0) / 0.2 * LOG2E
LEAF, RANK, VECS, LEAF_DEV, NEAR, FAR = 256, 64, 16, 32, 8, 6
ROWS = 32
PITCH = 9
CHUNKS = 4
GROUP = 4
NN = (((1,), (0,)), ((), ()))
NT = (((1,), (1,)), ((), ()))
SMEM = pl.BlockSpec(memory_space=pltpu.SMEM)
VMEM = pl.BlockSpec(memory_space=pltpu.VMEM)
HBM = pl.BlockSpec(memory_space=pltpu.HBM)


def dot(a, b, dims=NN):
    return lax.dot_general(a, b, dims, preferred_element_type=F32)


def pieces(x):
    hi = x.astype(BF)
    lo = (x - hi.astype(F32)).astype(BF)
    return jnp.concatenate([hi, lo], axis=0)


def folded(y):
    half = y.shape[0] // 2
    return y[:half] + y[half:]


def low_lanes(shape):
    return lax.broadcasted_iota(jnp.int32, shape, 1) < RANK


def joined(a, b):
    return jnp.where(low_lanes(a.shape), a, b)


def swapped(x):
    return pltpu.roll(x, RANK, 1)


def order_matrix(transposed):
    row = lax.broadcasted_iota(jnp.int32, (128, 128), 1 if transposed else 0)
    col = lax.broadcasted_iota(jnp.int32, (128, 128), 0 if transposed else 1)
    at = col % RANK
    source = jnp.where(at < 32, 2 * at, 2 * at - 63) + (col // RANK) * RANK
    return jnp.where(row == source, 1.0, 0.0).astype(BF)


def unpack_rows(load, tiles, block):
    for i in range(ROWS):
        x = load(i).astype(F32)
        tiles[0, pl.ds(i * PITCH, 8), :] = x[:8]
        tiles[1, pl.ds(i * PITCH, 8), :] = x[8:]
    for s in range(16):
        block(s, tiles[s // 8, pl.ds(s % 8, ROWS, stride=PITCH), :])


def pack_transfer(load, tiles, order, write):
    held = [None] * 16

    def keep(s, x):
        held[s] = x

    unpack_rows(load, tiles, keep)
    for s in range(16):
        x = dot(held[s].astype(BF), order)
        y = swapped(x)
        parent_odd = (s // 2) % 2
        rows = [y, x] if parent_odd else [x, y]
        write(s // 2, s % 2, jnp.concatenate(rows, axis=0).astype(BF))


def up_kernel(
    vec_in, basis_in, transfer_in, sk, dev, ee, xs, vec, basis, transfer, tiles, nat, sem
):
    copies = [
        pltpu.make_async_copy(transfer_in, transfer, sem.at[0]),
        pltpu.make_async_copy(vec_in, vec, sem.at[1]),
        pltpu.make_async_copy(basis_in, basis, sem.at[2]),
    ]
    for c in copies:
        c.start()
    order = order_matrix(False)
    copies[0].wait()

    def group(g, _):
        base = pl.multiple_of(g * 16, 16)

        def write(m, child, value):
            ee[g * 8 + m, pl.ds(child * RANK, RANK), :] = value

        pack_transfer(
            lambda i: transfer[pl.ds(base, 16), pl.ds(i * 128, 128)], tiles, order, write
        )
        return 0

    lax.fori_loop(0, 4, group, 0)
    copies[1].wait()
    for i in range(LEAF_DEV):
        xs[i] = pieces(vec[:, i * LEAF : (i + 1) * LEAF])
    copies[2].wait()
    for m in range(LEAF_DEV // 2):
        x = xs[2 * m : 2 * m + 2].reshape(64, LEAF)
        b = basis[2 * m : 2 * m + 2].reshape(128, LEAF)
        r = dot(x, b, NT)
        nat[m] = joined(folded(r[:32]), folded(r[32:]))
    for m in range(LEAF_DEV // 2):
        sk[16 + m] = folded(dot(pieces(nat[m]), order))
    half = LEAF_DEV // 2
    while half > 1:
        for m in range(half, 2 * half, 2):
            a = folded(dot(pieces(sk[m]), ee[m]))
            b = folded(dot(pieces(sk[m + 1]), ee[m + 1]))
            sk[m // 2] = joined(a, b)
        half = half // 2
    top = folded(dot(pieces(sk[1]), ee[1]))
    sk[0] = jnp.where(low_lanes(top.shape), 0.0, top)
    dev[...] = joined(swapped(top[:8]), top[8:])


def split3(v):
    h1 = v.astype(BF).astype(F32)
    h2 = (v - h1).astype(BF).astype(F32)
    return h1, h2, (v - h1 - h2).astype(BF).astype(F32)


def features(c):
    row = lax.broadcasted_iota(jnp.int32, c.shape, 0)
    low = row < 4
    s = jnp.where(row % 4 < 3, (c - 0.5) * SIGMA, 0.0)
    h1, h2, h3 = split3(s)
    size = jnp.sum(jnp.where(low, s * s, 0.0), axis=0, keepdims=True)
    n1, n2, n3 = split3(size)
    j1, j2, j3 = split3(size + JITTER_SQ * SIGMA * SIGMA)

    def rows(*values):
        x = jnp.zeros(c.shape, F32)
        for at, v in enumerate(values):
            x = jnp.where(row == at, v, x)
        return x

    cross = -2.0 * jnp.where(low, h1, h2)
    own = [cross, cross, -2.0 * jnp.where(low, h3, h1), rows(j1, j2, j3, 1.0, 1.0, 1.0)]
    partner = [h1, h2, jnp.where(low, h1, h3), rows(1.0, 1.0, 1.0, n1, n2, n3)]
    return jnp.concatenate(own, axis=0), jnp.concatenate(partner, axis=0)


def prepare_kernel(
    lists, counts, where, xs_own, wide_own, wide_before, wide_after, xs, partner, own, pairs, total
):
    first = (where[0] - 1) * LEAF_DEV

    def prepare(i, count):
        lanes = pl.ds(pl.multiple_of(i * LEAF, LEAF), LEAF)
        for at, wide in enumerate((wide_before, wide_own, wide_after)):
            slot = at * LEAF_DEV + i
            xs[slot] = xs_own[i] if at == 1 else pieces(wide[0:VECS, lanes])
            mine, theirs = features(wide[VECS : VECS + 8, lanes])
            partner[slot] = theirs.T.astype(BF)
            if at == 1:
                own[i] = mine.astype(BF)
        live = counts[i]
        for m in range(NEAR):
            pairs[count] = (lists[m, i] - first) * LEAF_DEV + i
            count = count + (m < live).astype(jnp.int32)
        return count

    count = lax.fori_loop(0, LEAF_DEV, prepare, jnp.int32(0))
    xs[3 * LEAF_DEV] = jnp.zeros((32, LEAF), BF)
    partner[3 * LEAF_DEV] = partner[LEAF_DEV]
    for g in range(GROUP):
        pairs[count + g] = 3 * LEAF_DEV * LEAF_DEV
    total[0] = (count + GROUP - 1) // GROUP


def near_kernel(chunk, pairs, total, xs, partner, own, *rest):
    out = rest[-1]
    if chunk == 0:
        out[...] = jnp.zeros_like(out)

    def step(i, _):
        for g in range(GROUP):
            code = pairs[i * GROUP + g]
            p = code // LEAF_DEV
            c = code % LEAF_DEV
            t = dot(partner[p], own[c])
            u = t * lax.rsqrt(t)
            k = (u + LOG2E) * jnp.exp2(-u)
            khi = k.astype(BF)
            klo = (k - khi.astype(F32)).astype(BF)
            x = xs[p]
            r = folded(dot(x, khi)) + dot(x[:VECS], klo)
            lanes = pl.ds(pl.multiple_of(c * LEAF, LEAF), LEAF)
            out[:, lanes] = out[:, lanes] + r
        return 0

    groups = total[0]
    lax.fori_loop(groups * chunk // CHUNKS, groups * (chunk + 1) // CHUNKS, step, 0)


def top_kernel(
    devices,
    lists,
    where,
    tiles_in,
    transfer,
    coupling,
    out,
    ee,
    q,
    tiles,
    blocks,
    raw,
    sem,
):
    d = where[0]
    levels = devices.bit_length() - 1
    order = order_matrix(False)
    nodes = [(devices + d) >> (levels - level) for level in range(levels + 1)]
    copies = [
        pltpu.make_async_copy(coupling.at[nodes[level]], raw.at[level], sem.at[level])
        for level in range(1, levels + 1)
    ]
    for c in copies:
        c.start()

    def group(g, _):
        base = pl.multiple_of(g * 16, 16)

        def write(m, child, value):
            ee[g * 8 + m, pl.ds(child * RANK, RANK), :] = value

        pack_transfer(
            lambda i: transfer[pl.ds(base, 16), pl.ds(i * 128, 128)], tiles, order, write
        )
        return 0

    lax.fori_loop(0, 2 * devices // 16, group, 0)

    def place(m, _):
        a = tiles_in[place_of(2 * m, d, devices)]
        b = tiles_in[place_of(2 * m + 1, d, devices)]
        q[devices // 2 + m, 0:8] = joined(a, swapped(b))
        q[devices // 2 + m, 8:16] = joined(swapped(a), b)
        return 0

    lax.fori_loop(0, devices // 2, place, 0, unroll=4)
    half = devices // 2

    def parents(m):
        a = folded(dot(pieces(q[m]), ee[m]))
        b = folded(dot(pieces(q[m + 1]), ee[m + 1]))
        return joined(a, b)

    while half >= 2:
        if half >= 16:

            def some(i, _, half=half):
                for u in range(4):
                    m = half + 8 * i + 2 * u
                    q[m // 2] = parents(m)
                return 0

            lax.fori_loop(0, half // 8, some, 0)
        else:
            for m in range(half, 2 * half, 2):
                q[m // 2] = parents(m)
        half = half // 2
    for c in copies:
        c.wait()
    own = []
    for level in range(1, levels + 1):
        a = nodes[level]
        x = raw[level].astype(F32)
        for i in range(ROWS):
            blocks[pl.ds(i * 8, 2), :] = x[:, i * 128 : (i + 1) * 128]
        rhs, lhs = [], []
        for k in range(2):
            c = blocks[pl.ds(k, ROWS, stride=8), :]
            rhs += [c, swapped(c)]
            slot = lists[k, a]
            v = q[slot // 2]
            lhs.append(jnp.where(slot % 2 == k, v, swapped(v)))
        r = dot(pieces(joined(*lhs)), jnp.concatenate(rhs, axis=0).astype(BF))
        r = folded(dot(pieces(folded(r)), order))
        odd = a % 2 == 1
        r = jnp.where(odd, swapped(r), r)
        own.append(jnp.where(low_lanes(r.shape) != odd, r, 0.0))
    path = own[0]
    for level in range(2, levels + 1):
        r = folded(dot(pieces(path), ee[nodes[level - 1]], NT))
        odd = nodes[level] % 2 == 1
        path = jnp.where(low_lanes(r.shape) != odd, r, 0.0) + own[level - 1]
    out[...] = jnp.where(nodes[levels] % 2 == 1, path, swapped(path))


def down_kernel(
    lists,
    where,
    sk_own,
    sk_before,
    sk_after,
    coupling,
    ee,
    basis,
    path,
    near,
    out,
    table,
    blocks,
    tiles,
    nat,
    field,
):
    slots = 2 * LEAF_DEV
    first = (where[0] - 1) * slots
    order = order_matrix(False)
    back = order_matrix(True)
    for at, sk in enumerate((sk_before, sk_own, sk_after)):

        def double(m, _):
            x = sk[m]
            y = swapped(x)
            table[at * slots + 2 * m] = pieces(joined(x, y))
            table[at * slots + 2 * m + 1] = pieces(joined(y, x))
            return 0

        lax.fori_loop(0, LEAF_DEV, double, 0, unroll=4)
    for k in range(FAR):

        def group(g, _):
            base = pl.multiple_of(g * 16, 16)

            def write(s, c):
                y = swapped(c)
                rows = [y, c] if s % 2 else [c, y]
                blocks[g * 16 + s, k * RANK : (k + 1) * RANK, :] = jnp.concatenate(
                    rows, axis=0
                ).astype(BF)

            unpack_rows(
                lambda i: coupling[k, pl.ds(base, 16), pl.ds(i * 128, 128)], tiles, write
            )
            return 0

        lax.fori_loop(0, slots // 16, group, 0)

    def couple(i, _):
        for u in range(4):
            m = jnp.maximum(4 * i + u, 1)
            sides = []
            for side in range(2):
                j = 2 * m + side
                parts = []
                for k in range(0, FAR, 2):
                    a = table[lists[k, j] - first]
                    b = table[lists[k + 1, j] - first]
                    parts.append(joined(a, b))
                sides.append(folded(dot(jnp.concatenate(parts, axis=1), blocks[j])))
            nat[m] = joined(*sides)
        return 0

    nat[0] = jnp.zeros((VECS, 128), F32)
    lax.fori_loop(0, LEAF_DEV // 4, couple, 0)
    for i in range(LEAF_DEV // 8):
        x = nat[8 * i : 8 * i + 8].reshape(8 * VECS, 128)
        x = folded(dot(pieces(x), order))
        field[8 * i : 8 * i + 8] = x.reshape(8, VECS, 128)
    field[0] = path[...]
    for m in range(1, LEAF_DEV):
        x = field[m // 2]
        x = jnp.where(low_lanes(x.shape) != (m % 2 == 1), x, 0.0)
        field[m] = field[m] + folded(dot(pieces(x), ee[m], NT))
    for m in range(LEAF_DEV // 2):
        x = folded(dot(pieces(field[LEAF_DEV // 2 + m]), back))
        low = low_lanes(x.shape)
        lhs = jnp.concatenate(
            [pieces(jnp.where(low, x, 0.0)), pieces(jnp.where(low, 0.0, x))], axis=0
        )
        r = dot(lhs, basis[2 * m : 2 * m + 2].reshape(128, LEAF))
        for side in range(2):
            lanes = slice((2 * m + side) * LEAF, (2 * m + side + 1) * LEAF)
            far = folded(r[32 * side : 32 * side + 32])
            out[:, lanes] = far + near[:, lanes] * (LN2 / math.sqrt(LEAF))


def call(kernel, out_shape, in_specs, scratch=(), name=None, us=1, out_specs=None, alias=None, mib=16):
    return pl.pallas_call(
        kernel,
        out_shape=out_shape,
        in_specs=in_specs,
        out_specs=jax.tree.map(lambda _: VMEM, out_shape) if out_specs is None else out_specs,
        scratch_shapes=list(scratch),
        compiler_params=pltpu.CompilerParams(vmem_limit_bytes=mib << 20),
        input_output_aliases=alias or {},
        name=name,
        cost_estimate=pl.CostEstimate(
            flops=us * 10**9, bytes_accessed=us * 10**6, transcendentals=0
        ),
    )


def shaped(shape, dtype=F32):
    return jax.ShapeDtypeStruct(shape, dtype)


def phases_of(devices):
    if devices == 128:
        return [(2, 4), (8, 4), (32, 4), (1, 2)]
    return [(1 << bit, 2) for bit in range(devices.bit_length() - 1)]


def exchanged(tile, stride, size, devices):
    got = [tile]
    for k in range(1, size):
        pairs = []
        for i in range(devices):
            at = i // stride % size
            pairs.append((i, i + ((at - k) % size - at) * stride))
        got.append(lax.ppermute(tile, AXES, pairs))
    return got


def place_of(i, position, devices):
    place, scale = 0, 1
    for stride, size in phases_of(devices):
        place = place + ((i // stride - position // stride) & (size - 1)) * scale
        scale = scale * size
    return place


def per_device(
    vectors,
    coords,
    leaf_basis,
    transfer,
    coupling,
    near_list,
    near_count,
    local_list,
    top_transfer,
    top_coupling,
    top_list,
):
    devices = lax.axis_size(AXES)
    position = lax.axis_index(AXES).astype(jnp.int32)
    where = position.reshape(1)
    up = [(i, i + 1) for i in range(devices - 1)]
    down = [(j, i) for i, j in up]
    blank = jnp.zeros((1, LEAF_DEV * LEAF), F32)
    wide = jnp.concatenate([vectors, coords, blank, coords, blank], axis=0)
    wide_before = lax.ppermute(wide, AXES, up)
    wide_after = lax.ppermute(wide, AXES, down)
    sk, dev, ee, xs = call(
        up_kernel,
        (
            shaped((LEAF_DEV, VECS, 128)),
            shaped((8, 128)),
            shaped((LEAF_DEV, 128, 128), BF),
            shaped((LEAF_DEV, 32, LEAF), BF),
        ),
        [HBM] * 3,
        [
            pltpu.VMEM((VECS, LEAF_DEV * LEAF), F32),
            pltpu.VMEM((LEAF_DEV, RANK, LEAF), BF),
            pltpu.VMEM((2 * LEAF_DEV, RANK * RANK), BF),
            pltpu.VMEM((2, PITCH * ROWS, 128), F32),
            pltpu.VMEM((16, VECS, 128), F32),
            pltpu.SemaphoreType.DMA((3,)),
        ],
        "up",
    )(vectors, leaf_basis, transfer)
    sk_before = lax.ppermute(sk, AXES, up)
    sk_after = lax.ppermute(sk, AXES, down)
    *tables, pairs, total = call(
        prepare_kernel,
        (
            shaped((3 * LEAF_DEV + 1, 32, LEAF), BF),
            shaped((3 * LEAF_DEV + 1, LEAF, 32), BF),
            shaped((LEAF_DEV, 32, LEAF), BF),
            shaped((LEAF_DEV * NEAR + GROUP,), jnp.int32),
            shaped((1,), jnp.int32),
        ),
        [SMEM] * 3 + [VMEM] * 4,
        (),
        "prepare",
        us=4,
        out_specs=(VMEM, VMEM, VMEM, SMEM, SMEM),
        mib=24,
    )(near_list.T, near_count, where, xs, wide, wide_before, wide_after)
    near = ()
    phases = phases_of(devices)
    tiles = dev[None]
    for at in range(max(CHUNKS, len(phases))):
        got = exchanged(tiles, *phases[at], devices) if at < len(phases) else [tiles]
        if at < CHUNKS:
            near = (
                call(
                    functools.partial(near_kernel, at),
                    shaped((VECS, LEAF_DEV * LEAF)),
                    [SMEM] * 2 + [VMEM] * (3 + len(near)),
                    (),
                    "near%d" % at,
                    us=8,
                    alias={5: 0} if near else None,
                )(pairs, total, *tables, *near),
            )
        *got, held = lax.optimization_barrier((*got, near[0]))
        tiles = jnp.concatenate(got, axis=0)
        tiles, held = lax.optimization_barrier((tiles, held))
        near = (held,)
    levels = devices.bit_length() - 1
    path = call(
        functools.partial(top_kernel, devices),
        shaped((VECS, 128)),
        [SMEM] * 2 + [VMEM] * 2 + [HBM],
        [
            pltpu.VMEM((devices, 128, 128), BF),
            pltpu.VMEM((devices, VECS, 128), F32),
            pltpu.VMEM((2, PITCH * ROWS, 128), F32),
            pltpu.VMEM((256, 128), F32),
            pltpu.VMEM((levels + 1, 2, RANK * RANK), BF),
            pltpu.SemaphoreType.DMA((levels + 1,)),
        ],
        "top",
    )(top_list.T, where, tiles, top_transfer, top_coupling)
    return call(
        down_kernel,
        shaped((VECS, LEAF_DEV * LEAF)),
        [SMEM] * 2 + [VMEM] * 8,
        [
            pltpu.VMEM((6 * LEAF_DEV, 32, 128), BF),
            pltpu.VMEM((2 * LEAF_DEV, FAR * RANK, 128), BF),
            pltpu.VMEM((2, PITCH * ROWS, 128), F32),
            pltpu.VMEM((LEAF_DEV, VECS, 128), F32),
            pltpu.VMEM((LEAF_DEV, VECS, 128), F32),
        ],
        "down",
    )(
        local_list.T,
        where,
        sk,
        sk_before,
        sk_after,
        jnp.transpose(coupling, (1, 0, 2)),
        ee,
        leaf_basis,
        path,
        near[0],
    )


def solution(mesh):
    split = P(None, AXES)
    return jax.shard_map(
        per_device,
        mesh=mesh,
        in_specs=(
            split,
            split,
            P(AXES, None, None),
            P(AXES, None),
            P(AXES, None, None),
            P(AXES, None),
            P(AXES),
            P(AXES, None),
            P(),
            P(),
            P(),
        ),
        out_specs=split,
        check_vma=False,
    )
```

```python
import functools
import math

import jax
import jax.numpy as jnp
from jax import lax
from jax.experimental import pallas as pl
from jax.experimental.pallas import tpu as pltpu
from jax.sharding import PartitionSpec as P

AXES = ("row", "col")
BF = jnp.bfloat16
F32 = jnp.float32
LOG2E = 1.4426950408889634
LN2 = 0.6931471805599453
JITTER_SQ = 0.0001
SIGMA = math.sqrt(3.0) / 0.2 * LOG2E
LEAF, RANK, VECS, LEAF_DEV, NEAR, FAR = 256, 64, 16, 32, 8, 6
ROWS = 32
PITCH = 9
CHUNKS = 4
PAIRS = 384
GROUP = 4
NN = (((1,), (0,)), ((), ()))
NT = (((1,), (1,)), ((), ()))
SMEM = pl.BlockSpec(memory_space=pltpu.SMEM)
VMEM = pl.BlockSpec(memory_space=pltpu.VMEM)
HBM = pl.BlockSpec(memory_space=pltpu.HBM)


def dot(a, b, dims=NN):
    return lax.dot_general(a, b, dims, preferred_element_type=F32)


def pieces(x):
    hi = x.astype(BF)
    lo = (x - hi.astype(F32)).astype(BF)
    return jnp.concatenate([hi, lo], axis=0)


def folded(y):
    half = y.shape[0] // 2
    return y[:half] + y[half:]


def low_lanes(shape):
    return lax.broadcasted_iota(jnp.int32, shape, 1) < RANK


def joined(a, b):
    return jnp.where(low_lanes(a.shape), a, b)


def swapped(x):
    return pltpu.roll(x, RANK, 1)


def order_matrix(transposed):
    row = lax.broadcasted_iota(jnp.int32, (128, 128), 1 if transposed else 0)
    col = lax.broadcasted_iota(jnp.int32, (128, 128), 0 if transposed else 1)
    at = col % RANK
    source = jnp.where(at < 32, 2 * at, 2 * at - 63) + (col // RANK) * RANK
    return jnp.where(row == source, 1.0, 0.0).astype(BF)


def unpack_rows(load, tiles, block):
    for i in range(ROWS):
        x = load(i).astype(F32)
        tiles[0, pl.ds(i * PITCH, 8), :] = x[:8]
        tiles[1, pl.ds(i * PITCH, 8), :] = x[8:]
    for s in range(16):
        block(s, tiles[s // 8, pl.ds(s % 8, ROWS, stride=PITCH), :])


def pack_transfer(load, tiles, order, write):
    held = [None] * 16

    def keep(s, x):
        held[s] = x

    unpack_rows(load, tiles, keep)
    for s in range(16):
        x = dot(held[s].astype(BF), order)
        y = swapped(x)
        parent_odd = (s // 2) % 2
        rows = [y, x] if parent_odd else [x, y]
        write(s // 2, s % 2, jnp.concatenate(rows, axis=0).astype(BF))


def pair_list(lists, counts, first):
    shape = lists.shape
    partner = lists - first
    live = lax.broadcasted_iota(jnp.int32, shape, 0) < counts
    local = live & (partner >= LEAF_DEV) & (partner < 2 * LEAF_DEV)
    before = lax.broadcasted_iota(jnp.int32, (LEAF_DEV, LEAF_DEV), 0)
    before = before < lax.broadcasted_iota(jnp.int32, (LEAF_DEV, LEAF_DEV), 1)
    above = lax.broadcasted_iota(jnp.int32, (NEAR, NEAR), 1)
    above = above < lax.broadcasted_iota(jnp.int32, (NEAR, NEAR), 0)

    def ranks(mask):
        flag = jnp.where(mask, 1.0, 0.0)
        line = jnp.broadcast_to(jnp.sum(flag, axis=1, keepdims=True), shape)
        rank = dot(flag.astype(BF), jnp.where(before, 1.0, 0.0).astype(BF))
        rank += dot(jnp.where(above, 1.0, 0.0).astype(BF), line.astype(BF))
        return rank, jnp.sum(jnp.sum(flag, axis=1, keepdims=True), axis=0, keepdims=True)

    rank_local, n_local = ranks(local)
    rank_other, n_other = ranks(live & ~local)
    rank = jnp.where(local, rank_local, jnp.where(live, rank_other + n_local, -1.0))
    rank = jnp.concatenate([rank, jnp.zeros((NEAR, 128 - LEAF_DEV), F32)], axis=1).T
    slot = lax.broadcasted_iota(jnp.int32, (LEAF_DEV, PAIRS), 1).astype(F32)
    row = lax.broadcasted_iota(jnp.int32, shape, 0)
    leaf = lax.broadcasted_iota(jnp.int32, shape, 1).astype(F32)
    known = jnp.where(live, partner, 0).astype(F32)
    found = jnp.zeros((NEAR, PAIRS), F32)
    for m in range(NEAR):
        hit = jnp.where(rank[:LEAF_DEV, m : m + 1] == slot, 1.0, 0.0).astype(BF)
        what = jnp.where(row == 0, known[m : m + 1], jnp.where(row == 1, leaf, 1.0))
        found += dot(what.astype(BF), hit)
    code = jnp.where(found[2:3] > 0.5, found[0:1] * LEAF_DEV + found[1:2], 3.0 * LEAF_DEV**2)
    at = lax.broadcasted_iota(jnp.int32, code.shape, 1)
    code = jnp.where(at == PAIRS - 2, n_local, code)
    return jnp.where(at == PAIRS - 1, n_local + n_other, code).astype(jnp.int32)


def up_kernel(
    lists,
    counts,
    where,
    vec_in,
    coords_in,
    basis_in,
    transfer_in,
    sk,
    dev,
    ee,
    xs,
    wide,
    pairs,
    coords,
    basis,
    transfer,
    tiles,
    nat,
    sem,
):
    copies = [
        pltpu.make_async_copy(transfer_in, transfer, sem.at[0]),
        pltpu.make_async_copy(vec_in, wide.at[pl.ds(0, VECS)], sem.at[1]),
        pltpu.make_async_copy(basis_in, basis, sem.at[2]),
        pltpu.make_async_copy(coords_in, coords, sem.at[3]),
    ]
    for c in copies:
        c.start()
    order = order_matrix(False)
    copies[0].wait()

    def group(g, _):
        base = pl.multiple_of(g * 16, 16)

        def write(m, child, value):
            ee[g * 8 + m, pl.ds(child * RANK, RANK), :] = value

        pack_transfer(
            lambda i: transfer[pl.ds(base, 16), pl.ds(i * 128, 128)], tiles, order, write
        )
        return 0

    lax.fori_loop(0, 4, group, 0)
    copies[1].wait()
    copies[3].wait()
    pairs[...] = pair_list(lists[...], counts[...], (where[0] - 1) * LEAF_DEV)
    for i in range(LEAF_DEV):
        lanes = slice(i * LEAF, (i + 1) * LEAF)
        xs[i] = pieces(wide[0:VECS, lanes])
        c = coords[:, lanes]
        blank = jnp.zeros((1, LEAF), F32)
        wide[VECS : VECS + 8, lanes] = jnp.concatenate([c, blank, c, blank], axis=0)
    copies[2].wait()
    for m in range(LEAF_DEV // 2):
        x = xs[2 * m : 2 * m + 2].reshape(64, LEAF)
        b = basis[2 * m : 2 * m + 2].reshape(128, LEAF)
        r = dot(x, b, NT)
        nat[m] = joined(folded(r[:32]), folded(r[32:]))
    for m in range(LEAF_DEV // 2):
        sk[16 + m] = folded(dot(pieces(nat[m]), order))
    half = LEAF_DEV // 2
    while half > 1:
        for m in range(half, 2 * half, 2):
            a = folded(dot(pieces(sk[m]), ee[m]))
            b = folded(dot(pieces(sk[m + 1]), ee[m + 1]))
            sk[m // 2] = joined(a, b)
        half = half // 2
    top = folded(dot(pieces(sk[1]), ee[1]))
    sk[0] = jnp.where(low_lanes(top.shape), 0.0, top)
    dev[...] = joined(swapped(top[:8]), top[8:])


def split3(v):
    h1 = v.astype(BF).astype(F32)
    h2 = (v - h1).astype(BF).astype(F32)
    return h1, h2, (v - h1 - h2).astype(BF).astype(F32)


def features(c):
    row = lax.broadcasted_iota(jnp.int32, c.shape, 0)
    low = row < 4
    s = jnp.where(row % 4 < 3, (c - 0.5) * SIGMA, 0.0)
    h1, h2, h3 = split3(s)
    size = jnp.sum(jnp.where(low, s * s, 0.0), axis=0, keepdims=True)
    n1, n2, n3 = split3(size)
    j1, j2, j3 = split3(size + JITTER_SQ * SIGMA * SIGMA)

    def rows(*values):
        x = jnp.zeros(c.shape, F32)
        for at, v in enumerate(values):
            x = jnp.where(row == at, v, x)
        return x

    cross = -2.0 * jnp.where(low, h1, h2)
    own = [cross, cross, -2.0 * jnp.where(low, h3, h1), rows(j1, j2, j3, 1.0, 1.0, 1.0)]
    partner = [h1, h2, jnp.where(low, h1, h3), rows(1.0, 1.0, 1.0, n1, n2, n3)]
    return jnp.concatenate(own, axis=0), jnp.concatenate(partner, axis=0)


def four_leaves(c):
    own, partner = features(c)
    parts = [partner[:, q * LEAF : (q + 1) * LEAF] for q in range(4)]
    return own.astype(BF), jnp.concatenate(parts, axis=0).T.astype(BF)


def own_kernel(wide, partner, own):
    def prepare(i, _):
        lanes = pl.ds(pl.multiple_of(i * 4 * LEAF, 4 * LEAF), 4 * LEAF)
        mine, partner[i] = four_leaves(wide[VECS : VECS + 8, lanes])
        for q in range(4):
            own[4 * i + q, 0:96] = jnp.zeros((96, LEAF), BF)
            own[4 * i + q, 96:128] = mine[:, q * LEAF : (q + 1) * LEAF]
            own[4 * i + q, 128:224] = jnp.zeros((96, LEAF), BF)
        return 0

    lax.fori_loop(0, LEAF_DEV // 4, prepare, 0)


def other_kernel(xs_own, partner_own, before, after, xs, partner):
    xs[pl.ds(LEAF_DEV, LEAF_DEV)] = xs_own[...]
    xs[3 * LEAF_DEV] = jnp.zeros((32, LEAF), BF)
    partner[pl.ds(LEAF_DEV // 4, LEAF_DEV // 4)] = partner_own[...]
    partner[3 * LEAF_DEV // 4] = partner_own[0]

    def prepare(i, _):
        for at, wide in ((0, before), (2, after)):
            for q in range(4):
                lanes = pl.ds(pl.multiple_of((4 * i + q) * LEAF, LEAF), LEAF)
                xs[at * LEAF_DEV + 4 * i + q] = pieces(wide[0:VECS, lanes])
            lanes = pl.ds(pl.multiple_of(i * 4 * LEAF, 4 * LEAF), 4 * LEAF)
            _, partner[at * LEAF_DEV // 4 + i] = four_leaves(wide[VECS : VECS + 8, lanes])
        return 0

    lax.fori_loop(0, LEAF_DEV // 4, prepare, 0, unroll=2)


def near_kernel(chunk, pairs, xs, partner, own, *rest):
    out = rest[-1]
    groups = (pairs[0, PAIRS - 1] + GROUP - 1) // GROUP
    start = jnp.minimum(groups // CHUNKS, pairs[0, PAIRS - 2] // GROUP)
    if chunk == 0:
        out[...] = jnp.zeros_like(out)
        begin, end, skip = 0, start, LEAF_DEV
    else:
        out[...] = rest[0][...]
        begin = start + (groups - start) * (chunk - 1) // (CHUNKS - 1)
        end = start + (groups - start) * chunk // (CHUNKS - 1)
        skip = 0

    def step(i, _):
        for g in range(GROUP):
            code = pairs[0, i * GROUP + g]
            p = (code >> 5) - skip
            c = code & (LEAF_DEV - 1)
            rows = pl.ds(pl.multiple_of(96 - (p & 3) * 32, 32), 128)
            t = dot(partner[p >> 2], own[c, rows, :])
            u = t * lax.rsqrt(t)
            k = (u + LOG2E) * jnp.exp2(-u)
            khi = k.astype(BF)
            klo = (k - khi.astype(F32)).astype(BF)
            x = xs[p]
            r = folded(dot(x, khi)) + dot(x[:VECS], klo)
            lanes = pl.ds(pl.multiple_of(c * LEAF, LEAF), LEAF)
            out[:, lanes] = out[:, lanes] + r
        return 0

    lax.fori_loop(begin, end, step, 0)


def top_kernel(
    devices,
    lists,
    where,
    tiles_in,
    transfer,
    coupling,
    out,
    ee,
    q,
    tiles,
    blocks,
    raw,
    sem,
):
    d = where[0]
    levels = devices.bit_length() - 1
    order = order_matrix(False)
    nodes = [(devices + d) >> (levels - level) for level in range(levels + 1)]
    copies = [
        pltpu.make_async_copy(coupling.at[nodes[level]], raw.at[level], sem.at[level])
        for level in range(1, levels + 1)
    ]
    for c in copies:
        c.start()

    def group(g, _):
        base = pl.multiple_of(g * 16, 16)

        def write(m, child, value):
            ee[g * 8 + m, pl.ds(child * RANK, RANK), :] = value

        pack_transfer(
            lambda i: transfer[pl.ds(base, 16), pl.ds(i * 128, 128)], tiles, order, write
        )
        return 0

    lax.fori_loop(0, 2 * devices // 16, group, 0)

    def place(m, _):
        a = tiles_in[place_of(2 * m, d, devices)]
        b = tiles_in[place_of(2 * m + 1, d, devices)]
        q[devices // 2 + m, 0:8] = joined(a, swapped(b))
        q[devices // 2 + m, 8:16] = joined(swapped(a), b)
        return 0

    lax.fori_loop(0, devices // 2, place, 0, unroll=4)
    half = devices // 2

    def parents(m):
        a = folded(dot(pieces(q[m]), ee[m]))
        b = folded(dot(pieces(q[m + 1]), ee[m + 1]))
        return joined(a, b)

    while half >= 2:
        if half >= 16:

            def some(i, _, half=half):
                for u in range(4):
                    m = half + 8 * i + 2 * u
                    q[m // 2] = parents(m)
                return 0

            lax.fori_loop(0, half // 8, some, 0)
        else:
            for m in range(half, 2 * half, 2):
                q[m // 2] = parents(m)
        half = half // 2
    for c in copies:
        c.wait()
    own = []
    for level in range(1, levels + 1):
        a = nodes[level]
        x = raw[level].astype(F32)
        for i in range(ROWS):
            blocks[pl.ds(i * 8, 2), :] = x[:, i * 128 : (i + 1) * 128]
        rhs, lhs = [], []
        for k in range(2):
            c = blocks[pl.ds(k, ROWS, stride=8), :]
            rhs += [c, swapped(c)]
            slot = lists[k, a]
            v = q[slot // 2]
            lhs.append(jnp.where(slot % 2 == k, v, swapped(v)))
        r = dot(pieces(joined(*lhs)), jnp.concatenate(rhs, axis=0).astype(BF))
        r = folded(dot(pieces(folded(r)), order))
        odd = a % 2 == 1
        r = jnp.where(odd, swapped(r), r)
        own.append(jnp.where(low_lanes(r.shape) != odd, r, 0.0))
    path = own[0]
    for level in range(2, levels + 1):
        r = folded(dot(pieces(path), ee[nodes[level - 1]], NT))
        odd = nodes[level] % 2 == 1
        path = jnp.where(low_lanes(r.shape) != odd, r, 0.0) + own[level - 1]
    out[...] = jnp.where(nodes[levels] % 2 == 1, path, swapped(path))


def down_kernel(
    lists,
    where,
    sk_own,
    sk_before,
    sk_after,
    coupling,
    ee,
    basis,
    path,
    near,
    out,
    table,
    blocks,
    tiles,
    nat,
    field,
):
    slots = 2 * LEAF_DEV
    first = (where[0] - 1) * slots
    order = order_matrix(False)
    back = order_matrix(True)
    for at, sk in enumerate((sk_before, sk_own, sk_after)):

        def double(m, _):
            x = sk[m]
            y = swapped(x)
            table[at * slots + 2 * m] = pieces(joined(x, y))
            table[at * slots + 2 * m + 1] = pieces(joined(y, x))
            return 0

        lax.fori_loop(0, LEAF_DEV, double, 0, unroll=4)
    for k in range(FAR):

        def group(g, _):
            base = pl.multiple_of(g * 16, 16)

            def write(s, c):
                y = swapped(c)
                rows = [y, c] if s % 2 else [c, y]
                blocks[g * 16 + s, k * RANK : (k + 1) * RANK, :] = jnp.concatenate(
                    rows, axis=0
                ).astype(BF)

            unpack_rows(
                lambda i: coupling[k, pl.ds(base, 16), pl.ds(i * 128, 128)], tiles, write
            )
            return 0

        lax.fori_loop(0, slots // 16, group, 0)

    def couple(i, _):
        for u in range(4):
            m = jnp.maximum(4 * i + u, 1)
            sides = []
            for side in range(2):
                j = 2 * m + side
                parts = []
                for k in range(0, FAR, 2):
                    a = table[lists[k, j] - first]
                    b = table[lists[k + 1, j] - first]
                    parts.append(joined(a, b))
                sides.append(folded(dot(jnp.concatenate(parts, axis=1), blocks[j])))
            nat[m] = joined(*sides)
        return 0

    nat[0] = jnp.zeros((VECS, 128), F32)
    lax.fori_loop(0, LEAF_DEV // 4, couple, 0)
    for i in range(LEAF_DEV // 8):
        x = nat[8 * i : 8 * i + 8].reshape(8 * VECS, 128)
        x = folded(dot(pieces(x), order))
        field[8 * i : 8 * i + 8] = x.reshape(8, VECS, 128)
    field[0] = path[...]
    for m in range(1, LEAF_DEV):
        x = field[m // 2]
        x = jnp.where(low_lanes(x.shape) != (m % 2 == 1), x, 0.0)
        field[m] = field[m] + folded(dot(pieces(x), ee[m], NT))
    for m in range(LEAF_DEV // 2):
        x = folded(dot(pieces(field[LEAF_DEV // 2 + m]), back))
        low = low_lanes(x.shape)
        lhs = jnp.concatenate(
            [pieces(jnp.where(low, x, 0.0)), pieces(jnp.where(low, 0.0, x))], axis=0
        )
        r = dot(lhs, basis[2 * m : 2 * m + 2].reshape(128, LEAF))
        for side in range(2):
            lanes = slice((2 * m + side) * LEAF, (2 * m + side + 1) * LEAF)
            far = folded(r[32 * side : 32 * side + 32])
            out[:, lanes] = far + near[:, lanes] * (LN2 / math.sqrt(LEAF))


def call(kernel, out_shape, in_specs, scratch=(), name=None, us=1, mib=16):
    return pl.pallas_call(
        kernel,
        out_shape=out_shape,
        in_specs=in_specs,
        out_specs=jax.tree.map(lambda _: VMEM, out_shape),
        scratch_shapes=list(scratch),
        compiler_params=pltpu.CompilerParams(vmem_limit_bytes=mib << 20),
        name=name,
        cost_estimate=pl.CostEstimate(
            flops=us * 10**9, bytes_accessed=us * 10**6, transcendentals=0
        ),
    )


def shaped(shape, dtype=F32):
    return jax.ShapeDtypeStruct(shape, dtype)


def phases_of(devices):
    if devices == 128:
        return [(2, 4), (8, 4), (32, 4), (1, 2)]
    return [(1 << bit, 2) for bit in range(devices.bit_length() - 1)]


def exchanged(tile, stride, size, devices):
    got = [tile]
    for k in range(1, size):
        pairs = []
        for i in range(devices):
            at = i // stride % size
            pairs.append((i, i + ((at - k) % size - at) * stride))
        got.append(lax.ppermute(tile, AXES, pairs))
    return got


def place_of(i, position, devices):
    place, scale = 0, 1
    for stride, size in phases_of(devices):
        place = place + (((i >> stride.bit_length() - 1) - (position >> stride.bit_length() - 1)) & (size - 1)) * scale
        scale = scale * size
    return place


def per_device(
    vectors,
    coords,
    leaf_basis,
    transfer,
    coupling,
    near_list,
    near_count,
    local_list,
    top_transfer,
    top_coupling,
    top_list,
):
    devices = lax.axis_size(AXES)
    position = lax.axis_index(AXES).astype(jnp.int32)
    where = position.reshape(1)
    up = [(i, i + 1) for i in range(devices - 1)]
    down = [(j, i) for i, j in up]
    sk, dev, ee, xs_own, wide, pairs = call(
        up_kernel,
        (
            shaped((LEAF_DEV, VECS, 128)),
            shaped((8, 128)),
            shaped((LEAF_DEV, 128, 128), BF),
            shaped((LEAF_DEV, 32, LEAF), BF),
            shaped((24, LEAF_DEV * LEAF)),
            shaped((1, PAIRS), jnp.int32),
        ),
        [VMEM] * 2 + [SMEM] + [HBM] * 4,
        [
            pltpu.VMEM((3, LEAF_DEV * LEAF), F32),
            pltpu.VMEM((LEAF_DEV, RANK, LEAF), BF),
            pltpu.VMEM((2 * LEAF_DEV, RANK * RANK), BF),
            pltpu.VMEM((2, PITCH * ROWS, 128), F32),
            pltpu.VMEM((16, VECS, 128), F32),
            pltpu.SemaphoreType.DMA((4,)),
        ],
        "up",
    )(
        near_list.T,
        near_count.reshape(1, LEAF_DEV),
        where,
        *(
            pltpu.with_memory_space_constraint(x, pltpu.HBM)
            for x in (vectors, coords, leaf_basis, transfer)
        ),
    )
    phases = phases_of(devices)
    got = exchanged(dev[None], *phases[0], devices)
    before = lax.ppermute(wide, AXES, up)
    after = lax.ppermute(wide, AXES, down)
    partner_own, own = call(
        own_kernel,
        (
            shaped((LEAF_DEV // 4, LEAF, 128), BF),
            shaped((LEAF_DEV, 224, LEAF), BF),
        ),
        [VMEM],
        (),
        "own",
        us=2,
        mib=8,
    )(wide)
    near = call(
        functools.partial(near_kernel, 0),
        shaped((VECS, LEAF_DEV * LEAF)),
        [SMEM] + [VMEM] * 3,
        (),
        "near0",
        us=8,
        mib=8,
    )(pairs, xs_own, partner_own, own)
    *got, near, sk_late = lax.optimization_barrier((*got, near, sk))
    sk_before = lax.ppermute(sk_late, AXES, up)
    sk_after = lax.ppermute(sk_late, AXES, down)
    tiles = jnp.concatenate(got, axis=0)
    tiles, before, after = lax.optimization_barrier((tiles, before, after))
    xs, partner = call(
        other_kernel,
        (
            shaped((3 * LEAF_DEV + 1, 32, LEAF), BF),
            shaped((3 * LEAF_DEV // 4 + 1, LEAF, 128), BF),
        ),
        [VMEM] * 4,
        (),
        "other",
        us=2,
        mib=8,
    )(xs_own, partner_own, before, after)
    for at in range(1, max(CHUNKS, len(phases))):
        got = exchanged(tiles, *phases[at], devices) if at < len(phases) else [tiles]
        if at < CHUNKS:
            near = call(
                functools.partial(near_kernel, at),
                shaped((VECS, LEAF_DEV * LEAF)),
                [SMEM] + [VMEM] * 4,
                (),
                "near%d" % at,
                us=8,
                mib=8,
            )(pairs, xs, partner, own, near)
        *got, near = lax.optimization_barrier((*got, near))
        tiles = jnp.concatenate(got, axis=0)
        tiles, near = lax.optimization_barrier((tiles, near))
    levels = devices.bit_length() - 1
    path = call(
        functools.partial(top_kernel, devices),
        shaped((VECS, 128)),
        [SMEM] * 2 + [VMEM] * 2 + [HBM],
        [
            pltpu.VMEM((devices, 128, 128), BF),
            pltpu.VMEM((devices, VECS, 128), F32),
            pltpu.VMEM((2, PITCH * ROWS, 128), F32),
            pltpu.VMEM((256, 128), F32),
            pltpu.VMEM((levels + 1, 2, RANK * RANK), BF),
            pltpu.SemaphoreType.DMA((levels + 1,)),
        ],
        "top",
    )(top_list.T, where, tiles, top_transfer, top_coupling)
    return call(
        down_kernel,
        shaped((VECS, LEAF_DEV * LEAF)),
        [SMEM] * 2 + [VMEM] * 8,
        [
            pltpu.VMEM((6 * LEAF_DEV, 32, 128), BF),
            pltpu.VMEM((2 * LEAF_DEV, FAR * RANK, 128), BF),
            pltpu.VMEM((2, PITCH * ROWS, 128), F32),
            pltpu.VMEM((LEAF_DEV, VECS, 128), F32),
            pltpu.VMEM((LEAF_DEV, VECS, 128), F32),
        ],
        "down",
    )(
        local_list.T,
        where,
        sk,
        sk_before,
        sk_after,
        jnp.transpose(coupling, (1, 0, 2)),
        ee,
        leaf_basis,
        path,
        near,
    )


def solution(mesh):
    split = P(None, AXES)
    return jax.shard_map(
        per_device,
        mesh=mesh,
        in_specs=(
            split,
            split,
            P(AXES, None, None),
            P(AXES, None),
            P(AXES, None, None),
            P(AXES, None),
            P(AXES),
            P(AXES, None),
            P(),
            P(),
            P(),
        ),
        out_specs=split,
        check_vma=False,
    )
```

```python
import functools
import math

import jax
import jax.numpy as jnp
from jax import lax
from jax.experimental import pallas as pl
from jax.experimental.pallas import tpu as pltpu
from jax.sharding import PartitionSpec as P

AXES = ("row", "col")
BF = jnp.bfloat16
F32 = jnp.float32
LOG2E = 1.4426950408889634
LN2 = 0.6931471805599453
JITTER_SQ = 0.0001
SIGMA = math.sqrt(3.0) / 0.2 * LOG2E
LEAF, RANK, VECS, LEAF_DEV, NEAR, FAR = 256, 64, 16, 32, 8, 6
DEVICES = 128
ROWS = 32
PITCH = 9
PAIRS = 384
GROUP = 12
NN = (((1,), (0,)), ((), ()))
NT = (((1,), (1,)), ((), ()))
SMEM = pl.BlockSpec(memory_space=pltpu.SMEM)
VMEM = pl.BlockSpec(memory_space=pltpu.VMEM)
HBM = pl.BlockSpec(memory_space=pltpu.HBM)


def dot(a, b, dims=NN):
    return lax.dot_general(a, b, dims, preferred_element_type=F32)


def pieces(x):
    hi = x.astype(BF)
    lo = (x - hi.astype(F32)).astype(BF)
    return jnp.concatenate([hi, lo], axis=0)


def folded(y):
    half = y.shape[0] // 2
    return y[:half] + y[half:]


def low_lanes(shape):
    return lax.broadcasted_iota(jnp.int32, shape, 1) < RANK


def joined(a, b):
    return jnp.where(low_lanes(a.shape), a, b)


def swapped(x):
    return pltpu.roll(x, RANK, 1)


def order_matrix(transposed):
    row = lax.broadcasted_iota(jnp.int32, (128, 128), 1 if transposed else 0)
    col = lax.broadcasted_iota(jnp.int32, (128, 128), 0 if transposed else 1)
    at = col % RANK
    source = jnp.where(at < 32, 2 * at, 2 * at - 63) + (col // RANK) * RANK
    return jnp.where(row == source, 1.0, 0.0).astype(BF)


def unpack_rows(load, tiles, block):
    for i in range(ROWS):
        x = load(i).astype(F32)
        tiles[0, pl.ds(i * PITCH, 8), :] = x[:8]
        tiles[1, pl.ds(i * PITCH, 8), :] = x[8:]
    for s in range(16):
        block(s, tiles[s // 8, pl.ds(s % 8, ROWS, stride=PITCH), :])


def pack_transfer(load, tiles, order, write):
    held = [None] * 16

    def keep(s, x):
        held[s] = x.astype(BF)

    unpack_rows(load, tiles, keep)
    ordered = dot(jnp.concatenate(held, axis=0), order)
    for s in range(16):
        x = ordered[s * ROWS : (s + 1) * ROWS]
        y = swapped(x)
        parent_odd = (s // 2) % 2
        rows = [y, x] if parent_odd else [x, y]
        write(s // 2, s % 2, jnp.concatenate(rows, axis=0).astype(BF))


def pack_kernel(first, transfer, ee, tiles):
    order = order_matrix(False)

    def group(g, _):
        base = pl.multiple_of(first + g * 16, 16)

        def write(m, child, value):
            ee[g * 8 + m, pl.ds(child * RANK, RANK), :] = value

        pack_transfer(
            lambda i: transfer[pl.ds(base, 16), pl.ds(i * 128, 128)], tiles, order, write
        )
        return 0

    lax.fori_loop(0, transfer.shape[0] // 32, group, 0)


def blocks_kernel(coupling, blocks, tiles):
    for k in range(FAR):

        def group(g, _):
            base = pl.multiple_of(g * 16, 16)

            def write(s, c):
                y = swapped(c)
                rows = [y, c] if s % 2 else [c, y]
                blocks[g * 16 + s, k * RANK : (k + 1) * RANK, :] = jnp.concatenate(
                    rows, axis=0
                ).astype(BF)

            unpack_rows(
                lambda i: coupling[k, pl.ds(base, 16), pl.ds(i * 128, 128)], tiles, write
            )
            return 0

        lax.fori_loop(0, 2 * LEAF_DEV // 16, group, 0)


def pair_list(lists, counts, first):
    shape = lists.shape
    partner = lists - first
    live = lax.broadcasted_iota(jnp.int32, shape, 0) < counts
    local = live & (partner >= LEAF_DEV) & (partner < 2 * LEAF_DEV)
    before = lax.broadcasted_iota(jnp.int32, (LEAF_DEV, LEAF_DEV), 0)
    before = before < lax.broadcasted_iota(jnp.int32, (LEAF_DEV, LEAF_DEV), 1)
    above = lax.broadcasted_iota(jnp.int32, (NEAR, NEAR), 1)
    above = above < lax.broadcasted_iota(jnp.int32, (NEAR, NEAR), 0)

    def ranks(mask):
        flag = jnp.where(mask, 1.0, 0.0)
        line = jnp.broadcast_to(jnp.sum(flag, axis=1, keepdims=True), shape)
        rank = dot(flag.astype(BF), jnp.where(before, 1.0, 0.0).astype(BF))
        rank += dot(jnp.where(above, 1.0, 0.0).astype(BF), line.astype(BF))
        return rank, jnp.sum(jnp.sum(flag, axis=1, keepdims=True), axis=0, keepdims=True)

    rank_local, n_local = ranks(local)
    rank_other, n_other = ranks(live & ~local)
    rank = jnp.where(local, rank_local, jnp.where(live, rank_other + n_local, -1.0))
    rank = jnp.concatenate([rank, jnp.zeros((NEAR, 128 - LEAF_DEV), F32)], axis=1).T
    slot = lax.broadcasted_iota(jnp.int32, (LEAF_DEV, PAIRS), 1).astype(F32)
    row = lax.broadcasted_iota(jnp.int32, shape, 0)
    leaf = lax.broadcasted_iota(jnp.int32, shape, 1).astype(F32)
    known = jnp.where(live, partner, 0).astype(F32)
    found = jnp.zeros((NEAR, PAIRS), F32)
    for m in range(NEAR):
        hit = jnp.where(rank[:LEAF_DEV, m : m + 1] == slot, 1.0, 0.0).astype(BF)
        what = jnp.where(row == 0, known[m : m + 1], jnp.where(row == 1, leaf, 1.0))
        found += dot(what.astype(BF), hit)
    code = jnp.where(found[2:3] > 0.5, found[0:1] * LEAF_DEV + found[1:2], 3.0 * LEAF_DEV**2)
    at = lax.broadcasted_iota(jnp.int32, code.shape, 1)
    code = jnp.where(at == PAIRS - 2, n_local, code)
    return jnp.where(at == PAIRS - 1, n_local + n_other, code).astype(jnp.int32)


def up_kernel(
    where,
    lists_in,
    counts_in,
    vec_in,
    coords_in,
    basis_in,
    transfer_in,
    sk,
    dev,
    ee,
    xs,
    wide,
    pairs,
    lists,
    counts,
    coords,
    basis,
    transfer,
    tiles,
    nat,
    sem,
):
    copies = [
        pltpu.make_async_copy(transfer_in, transfer, sem.at[0]),
        pltpu.make_async_copy(vec_in, wide.at[pl.ds(0, VECS)], sem.at[1]),
        pltpu.make_async_copy(basis_in, basis, sem.at[2]),
        pltpu.make_async_copy(coords_in, coords, sem.at[3]),
        pltpu.make_async_copy(lists_in, lists, sem.at[4]),
        pltpu.make_async_copy(counts_in, counts, sem.at[5]),
    ]
    for c in copies:
        c.start()
    order = order_matrix(False)
    copies[0].wait()

    def group(g, _):
        base = pl.multiple_of(g * 16, 16)

        def write(m, child, value):
            ee[g * 8 + m, pl.ds(child * RANK, RANK), :] = value

        pack_transfer(
            lambda i: transfer[pl.ds(base, 16), pl.ds(i * 128, 128)], tiles, order, write
        )
        return 0

    lax.fori_loop(0, 4, group, 0)
    copies[1].wait()
    for c in copies[3:]:
        c.wait()
    pairs[...] = pair_list(lists[...], counts[...], (where[0] - 1) * LEAF_DEV)
    for i in range(LEAF_DEV):
        lanes = slice(i * LEAF, (i + 1) * LEAF)
        xs[i] = pieces(wide[0:VECS, lanes])
        c = coords[:, lanes]
        blank = jnp.zeros((1, LEAF), F32)
        wide[VECS : VECS + 8, lanes] = jnp.concatenate([c, blank, c, blank], axis=0)
    copies[2].wait()
    for m in range(LEAF_DEV // 2):
        x = xs[2 * m : 2 * m + 2].reshape(64, LEAF)
        b = basis[2 * m : 2 * m + 2].reshape(128, LEAF)
        r = dot(x, b, NT)
        nat[m] = joined(folded(r[:32]), folded(r[32:]))
    for m in range(LEAF_DEV // 2):
        sk[16 + m] = folded(dot(pieces(nat[m]), order))
    half = LEAF_DEV // 2
    while half > 1:
        for m in range(half, 2 * half, 2):
            a = folded(dot(pieces(sk[m]), ee[m]))
            b = folded(dot(pieces(sk[m + 1]), ee[m + 1]))
            sk[m // 2] = joined(a, b)
        half = half // 2
    top = folded(dot(pieces(sk[1]), ee[1]))
    sk[0] = jnp.where(low_lanes(top.shape), 0.0, top)
    dev[...] = joined(swapped(top[:8]), top[8:])
    for m in range(LEAF_DEV):
        for h in range(2):
            lanes = slice((2 * m + h) * 128, (2 * m + h + 1) * 128)
            wide[24:32, lanes] = sk[m, 8 * h : 8 * h + 8]


def split3(v):
    h1 = v.astype(BF).astype(F32)
    h2 = (v - h1).astype(BF).astype(F32)
    return h1, h2, (v - h1 - h2).astype(BF).astype(F32)


def features(c):
    row = lax.broadcasted_iota(jnp.int32, c.shape, 0)
    low = row < 4
    s = jnp.where(row % 4 < 3, (c - 0.5) * SIGMA, 0.0)
    h1, h2, h3 = split3(s)
    size = jnp.sum(jnp.where(low, s * s, 0.0), axis=0, keepdims=True)
    n1, n2, n3 = split3(size)
    j1, j2, j3 = split3(size + JITTER_SQ * SIGMA * SIGMA)

    def rows(*values):
        x = jnp.zeros(c.shape, F32)
        for at, v in enumerate(values):
            x = jnp.where(row == at, v, x)
        return x

    cross = -2.0 * jnp.where(low, h1, h2)
    own = [cross, cross, -2.0 * jnp.where(low, h3, h1), rows(j1, j2, j3, 1.0, 1.0, 1.0)]
    partner = [h1, h2, jnp.where(low, h1, h3), rows(1.0, 1.0, 1.0, n1, n2, n3)]
    return jnp.concatenate(own, axis=0), jnp.concatenate(partner, axis=0)


def four_leaves(c):
    own, partner = features(c)
    parts = [partner[:, q * LEAF : (q + 1) * LEAF] for q in range(4)]
    return own.astype(BF), jnp.concatenate(parts, axis=0).T.astype(BF)


def own_kernel(wide, partner, own):
    def prepare(i, _):
        lanes = pl.ds(pl.multiple_of(i * 4 * LEAF, 4 * LEAF), 4 * LEAF)
        mine, partner[i] = four_leaves(wide[VECS : VECS + 8, lanes])
        for q in range(4):
            own[4 * i + q, 0:96] = jnp.zeros((96, LEAF), BF)
            own[4 * i + q, 96:128] = mine[:, q * LEAF : (q + 1) * LEAF]
            own[4 * i + q, 128:224] = jnp.zeros((96, LEAF), BF)
        return 0

    lax.fori_loop(0, LEAF_DEV // 4, prepare, 0)


def other_kernel(xs_own, partner_own, before, after, xs, partner):
    xs[pl.ds(LEAF_DEV, LEAF_DEV)] = xs_own[...]
    xs[3 * LEAF_DEV] = jnp.zeros((32, LEAF), BF)
    partner[pl.ds(LEAF_DEV // 4, LEAF_DEV // 4)] = partner_own[...]
    partner[3 * LEAF_DEV // 4] = partner_own[0]

    def prepare(i, _):
        for at, wide in ((0, before), (2, after)):
            for q in range(4):
                lanes = pl.ds(pl.multiple_of((4 * i + q) * LEAF, LEAF), LEAF)
                xs[at * LEAF_DEV + 4 * i + q] = pieces(wide[0:VECS, lanes])
            lanes = pl.ds(pl.multiple_of(i * 4 * LEAF, 4 * LEAF), 4 * LEAF)
            _, partner[at * LEAF_DEV // 4 + i] = four_leaves(wide[VECS : VECS + 8, lanes])
        return 0

    lax.fori_loop(0, LEAF_DEV // 4, prepare, 0, unroll=2)


def near_kernel(chunk, pairs, xs, partner, own, *rest):
    out = rest[-1]
    start = lax.div(pairs[0, PAIRS - 2], GROUP)
    if chunk == 0:
        out[...] = jnp.zeros_like(out)
        begin, end, skip = 0, start, LEAF_DEV
    else:
        out[...] = rest[0][...]
        begin, end, skip = start, lax.div(pairs[0, PAIRS - 1] + GROUP - 1, GROUP), 0

    def step(i, _):
        for g in range(GROUP):
            code = pairs[0, i * GROUP + g]
            p = (code >> 5) - skip
            c = code & (LEAF_DEV - 1)
            rows = pl.ds(pl.multiple_of(96 - (p & 3) * 32, 32), 128)
            t = dot(partner[p >> 2], own[c, rows, :])
            u = t * lax.rsqrt(t)
            k = (u + LOG2E) * jnp.exp2(-u)
            khi = k.astype(BF)
            klo = (k - khi.astype(F32)).astype(BF)
            x = xs[p]
            r = folded(dot(x, khi)) + dot(x[:VECS], klo)
            lanes = pl.ds(pl.multiple_of(c * LEAF, LEAF), LEAF)
            out[:, lanes] = out[:, lanes] + r
        return 0

    lax.fori_loop(begin, end, step, 0)


def top_kernel(lists, where, tiles_in, ee_low, ee_high, coupling, out, q, blocks, raw, sem):
    d = where[0]
    devices = DEVICES
    levels = devices.bit_length() - 1
    order = order_matrix(False)
    nodes = [(devices + d) >> (levels - level) for level in range(levels + 1)]
    copies = [
        pltpu.make_async_copy(coupling.at[nodes[level]], raw.at[level], sem.at[level])
        for level in range(1, levels + 1)
    ]
    for c in copies:
        c.start()
    core, z, x, y = d & 1, (d >> 1) & 3, (d >> 3) & 3, (d >> 5) & 3

    def place(j, _):
        base = 4 * (((j & 3) - x) & 3) + 16 * (((j >> 2) - y) & 3)
        for u in range(4):
            at = base + ((u - z) & 3)
            a = tiles_in[at + 64 * core]
            b = tiles_in[at + 64 - 64 * core]
            m = 4 * j + u
            q[devices // 2 + m, 0:8] = joined(a, swapped(b))
            q[devices // 2 + m, 8:16] = joined(swapped(a), b)
        return 0

    lax.fori_loop(0, devices // 8, place, 0)

    def matrix(m, half):
        return ee_high[m - devices // 2] if half == devices // 2 else ee_low[m]

    half = devices // 2

    def parents(m, half):
        a = folded(dot(pieces(q[m]), matrix(m, half)))
        b = folded(dot(pieces(q[m + 1]), matrix(m + 1, half)))
        return joined(a, b)

    while half >= 2:
        if half >= 16:

            def some(i, _, half=half):
                for u in range(4):
                    m = half + 8 * i + 2 * u
                    q[m // 2] = parents(m, half)
                return 0

            lax.fori_loop(0, half // 8, some, 0)
        else:
            for m in range(half, 2 * half, 2):
                q[m // 2] = parents(m, half)
        half = half // 2
    for c in copies:
        c.wait()
    own = []
    for level in range(1, levels + 1):
        a = nodes[level]
        x = raw[level].astype(F32)
        for i in range(ROWS):
            blocks[pl.ds(i * 8, 2), :] = x[:, i * 128 : (i + 1) * 128]
        rhs, lhs = [], []
        for k in range(2):
            c = blocks[pl.ds(k, ROWS, stride=8), :]
            rhs += [c, swapped(c)]
            slot = lists[k, a]
            v = q[slot // 2]
            lhs.append(jnp.where(slot % 2 == k, v, swapped(v)))
        r = dot(pieces(joined(*lhs)), jnp.concatenate(rhs, axis=0).astype(BF))
        r = folded(dot(pieces(folded(r)), order))
        odd = a % 2 == 1
        r = jnp.where(odd, swapped(r), r)
        own.append(jnp.where(low_lanes(r.shape) != odd, r, 0.0))
    path = own[0]
    for level in range(2, levels + 1):
        r = folded(dot(pieces(path), matrix(nodes[level - 1], 1 << level - 1), NT))
        odd = nodes[level] % 2 == 1
        path = jnp.where(low_lanes(r.shape) != odd, r, 0.0) + own[level - 1]
    out[...] = jnp.where(nodes[levels] % 2 == 1, path, swapped(path))


def down_kernel(
    lists, where, sk_own, before, after, blocks, ee, basis, path, near, out, table, nat, field
):
    slots = 2 * LEAF_DEV
    first = (where[0] - 1) * slots
    order = order_matrix(False)
    back = order_matrix(True)

    def double(m, _):
        lanes = pl.ds(pl.multiple_of(m * 256, 256), 256)
        for at, wide in enumerate((before, None, after)):
            if wide is None:
                x = sk_own[m]
            else:
                x = wide[24:32, lanes]
                x = jnp.concatenate([x[:, :128], x[:, 128:]], axis=0)
            y = swapped(x)
            table[at * slots + 2 * m] = pieces(joined(x, y))
            table[at * slots + 2 * m + 1] = pieces(joined(y, x))
        return 0

    lax.fori_loop(0, LEAF_DEV, double, 0, unroll=2)

    def couple(i, _):
        for u in range(4):
            m = jnp.maximum(4 * i + u, 1)
            sides = []
            for side in range(2):
                j = 2 * m + side
                parts = []
                for k in range(0, FAR, 2):
                    a = table[lists[k, j] - first]
                    b = table[lists[k + 1, j] - first]
                    parts.append(joined(a, b))
                sides.append(folded(dot(jnp.concatenate(parts, axis=1), blocks[j])))
            nat[m] = joined(*sides)
        return 0

    nat[0] = jnp.zeros((VECS, 128), F32)
    lax.fori_loop(0, LEAF_DEV // 4, couple, 0)
    for i in range(LEAF_DEV // 8):
        x = nat[8 * i : 8 * i + 8].reshape(8 * VECS, 128)
        x = folded(dot(pieces(x), order))
        field[8 * i : 8 * i + 8] = x.reshape(8, VECS, 128)
    field[0] = path[...]
    for m in range(1, LEAF_DEV):
        x = field[m // 2]
        x = jnp.where(low_lanes(x.shape) != (m % 2 == 1), x, 0.0)
        field[m] = field[m] + folded(dot(pieces(x), ee[m], NT))
    for m in range(LEAF_DEV // 2):
        x = folded(dot(pieces(field[LEAF_DEV // 2 + m]), back))
        low = low_lanes(x.shape)
        lhs = jnp.concatenate(
            [pieces(jnp.where(low, x, 0.0)), pieces(jnp.where(low, 0.0, x))], axis=0
        )
        r = dot(lhs, basis[2 * m : 2 * m + 2].reshape(128, LEAF))
        for side in range(2):
            lanes = slice((2 * m + side) * LEAF, (2 * m + side + 1) * LEAF)
            far = folded(r[32 * side : 32 * side + 32])
            out[:, lanes] = far + near[:, lanes] * (LN2 / math.sqrt(LEAF))


def call(kernel, out_shape, in_specs, scratch=(), name=None, us=1, mib=16):
    return pl.pallas_call(
        kernel,
        out_shape=out_shape,
        in_specs=in_specs,
        out_specs=jax.tree.map(lambda _: VMEM, out_shape),
        scratch_shapes=list(scratch),
        compiler_params=pltpu.CompilerParams(vmem_limit_bytes=mib << 20),
        name=name,
        cost_estimate=pl.CostEstimate(
            flops=us * 10**9, bytes_accessed=us * 10**6, transcendentals=0
        ),
    )


def shaped(shape, dtype=F32):
    return jax.ShapeDtypeStruct(shape, dtype)


PHASES = ((2, 4), (8, 4), (32, 4), (1, 2))


def exchanged(tile, stride, size, devices):
    got = [tile]
    for k in range(1, size):
        pairs = []
        for i in range(devices):
            at = i // stride % size
            pairs.append((i, i + ((at - k) % size - at) * stride))
        got.append(lax.ppermute(tile, AXES, pairs))
    return got


def per_device(
    vectors,
    coords,
    leaf_basis,
    transfer,
    coupling,
    near_list,
    near_count,
    local_list,
    top_transfer,
    top_coupling,
    top_list,
):
    devices = lax.axis_size(AXES)
    position = lax.axis_index(AXES).astype(jnp.int32)
    where = position.reshape(1)
    up = [(i, i + 1) for i in range(devices - 1)]
    down = [(j, i) for i, j in up]
    sk, dev, ee, xs_own, wide, pairs = call(
        up_kernel,
        (
            shaped((LEAF_DEV, VECS, 128)),
            shaped((8, 128)),
            shaped((LEAF_DEV, 128, 128), BF),
            shaped((LEAF_DEV, 32, LEAF), BF),
            shaped((32, LEAF_DEV * LEAF)),
            shaped((1, PAIRS), jnp.int32),
        ),
        [SMEM] + [HBM] * 6,
        [
            pltpu.VMEM((NEAR, LEAF_DEV), jnp.int32),
            pltpu.VMEM((1, LEAF_DEV), jnp.int32),
            pltpu.VMEM((3, LEAF_DEV * LEAF), F32),
            pltpu.VMEM((LEAF_DEV, RANK, LEAF), BF),
            pltpu.VMEM((2 * LEAF_DEV, RANK * RANK), BF),
            pltpu.VMEM((2, PITCH * ROWS, 128), F32),
            pltpu.VMEM((16, VECS, 128), F32),
            pltpu.SemaphoreType.DMA((6,)),
        ],
        "up",
    )(
        where,
        *(
            pltpu.with_memory_space_constraint(x, pltpu.HBM)
            for x in (
                near_list.T,
                near_count.reshape(1, LEAF_DEV),
                vectors,
                coords,
                leaf_basis,
                transfer,
            )
        ),
    )
    order_scratch = [pltpu.VMEM((2, PITCH * ROWS, 128), F32)]

    def pack(x, first, name):
        return call(
            functools.partial(pack_kernel, first),
            shaped((devices // 2, 128, 128), BF),
            [VMEM],
            order_scratch,
            name,
            us=3,
        )(x)

    tied = lax.optimization_barrier
    got = exchanged(dev[None], *PHASES[0], devices)
    upper, _ = tied((top_transfer, dev))
    ee_low = pack(upper, 0, "pack0")
    *got, ee_low = tied((*got, ee_low))
    tiles = jnp.concatenate(got, axis=0)
    got = exchanged(tiles, *PHASES[1], devices)
    upper, _ = tied((top_transfer, tiles))
    ee_high = pack(upper, devices, "pack1")
    *got, ee_high = tied((*got, ee_high))
    tiles = jnp.concatenate(got, axis=0)
    got = exchanged(tiles, *PHASES[2], devices)
    stored, _ = tied((coupling, tiles))
    blocks = call(
        blocks_kernel,
        shaped((2 * LEAF_DEV, FAR * RANK, 128), BF),
        [VMEM],
        order_scratch,
        "blocks",
        us=3,
    )(jnp.transpose(stored, (1, 0, 2)))
    *got, blocks = tied((*got, blocks))
    tiles = jnp.concatenate(got, axis=0)
    got = exchanged(tiles, *PHASES[3], devices)
    wide_up, _ = tied((wide, tiles))
    before = lax.ppermute(wide_up, AXES, up)
    partner_own, own = call(
        own_kernel,
        (
            shaped((LEAF_DEV // 4, LEAF, 128), BF),
            shaped((LEAF_DEV, 224, LEAF), BF),
        ),
        [VMEM],
        (),
        "own",
        us=2,
    )(wide_up)
    *got, own = tied((*got, own))
    tiles = jnp.concatenate(got, axis=0)
    wide_down, _ = tied((wide, tiles))
    after = lax.ppermute(wide_down, AXES, down)
    levels = devices.bit_length() - 1
    path = call(
        top_kernel,
        shaped((VECS, 128)),
        [SMEM] * 2 + [VMEM] * 3 + [HBM],
        [
            pltpu.VMEM((devices, VECS, 128), F32),
            pltpu.VMEM((256, 128), F32),
            pltpu.VMEM((levels + 1, 2, RANK * RANK), BF),
            pltpu.SemaphoreType.DMA((levels + 1,)),
        ],
        "top",
        us=6,
    )(
        top_list.T,
        where,
        tiles,
        ee_low,
        ee_high,
        pltpu.with_memory_space_constraint(top_coupling, pltpu.HBM),
    )
    near = call(
        functools.partial(near_kernel, 0),
        shaped((VECS, LEAF_DEV * LEAF)),
        [SMEM] + [VMEM] * 3,
        (),
        "near0",
        us=8,
    )(pairs, xs_own, partner_own, own)
    near, before, after, path = tied((near, before, after, path))
    xs, partner = call(
        other_kernel,
        (
            shaped((3 * LEAF_DEV + 1, 32, LEAF), BF),
            shaped((3 * LEAF_DEV // 4 + 1, LEAF, 128), BF),
        ),
        [VMEM] * 4,
        (),
        "other",
        us=2,
    )(xs_own, partner_own, before, after)
    near = call(
        functools.partial(near_kernel, 1),
        shaped((VECS, LEAF_DEV * LEAF)),
        [SMEM] + [VMEM] * 4,
        (),
        "near1",
        us=8,
    )(pairs, xs, partner, own, near)
    return call(
        down_kernel,
        shaped((VECS, LEAF_DEV * LEAF)),
        [SMEM] * 2 + [VMEM] * 8,
        [
            pltpu.VMEM((6 * LEAF_DEV, 32, 128), BF),
            pltpu.VMEM((LEAF_DEV, VECS, 128), F32),
            pltpu.VMEM((LEAF_DEV, VECS, 128), F32),
        ],
        "down",
    )(local_list.T, where, sk, before, after, blocks, ee, leaf_basis, path, near)


def solution(mesh):
    split = P(None, AXES)
    return jax.shard_map(
        per_device,
        mesh=mesh,
        in_specs=(
            split,
            split,
            P(AXES, None, None),
            P(AXES, None),
            P(AXES, None, None),
            P(AXES, None),
            P(AXES),
            P(AXES, None),
            P(),
            P(),
            P(),
        ),
        out_specs=split,
        check_vma=False,
    )
```

```python
import functools
import math

import jax
import jax.numpy as jnp
from jax import lax
from jax.experimental import pallas as pl
from jax.experimental.pallas import tpu as pltpu
from jax.sharding import PartitionSpec as P

AXES = ("row", "col")
BF = jnp.bfloat16
F32 = jnp.float32
LOG2E = 1.4426950408889634
LN2 = 0.6931471805599453
JITTER_SQ = 0.0001
SIGMA = math.sqrt(3.0) / 0.2 * LOG2E
LEAF, RANK, VECS, LEAF_DEV, NEAR, FAR = 256, 64, 16, 32, 8, 6
DEVICES = 128
ROWS = 32
PITCH = 9
PAIRS = 384
GROUP = 12
NN = (((1,), (0,)), ((), ()))
NT = (((1,), (1,)), ((), ()))
SMEM = pl.BlockSpec(memory_space=pltpu.SMEM)
VMEM = pl.BlockSpec(memory_space=pltpu.VMEM)
HBM = pl.BlockSpec(memory_space=pltpu.HBM)


def dot(a, b, dims=NN):
    return lax.dot_general(a, b, dims, preferred_element_type=F32)


def pieces(x):
    hi = x.astype(BF)
    lo = (x - hi.astype(F32)).astype(BF)
    return jnp.concatenate([hi, lo], axis=0)


def folded(y):
    half = y.shape[0] // 2
    return y[:half] + y[half:]


def low_lanes(shape):
    return lax.broadcasted_iota(jnp.int32, shape, 1) < RANK


def joined(a, b):
    return jnp.where(low_lanes(a.shape), a, b)


def swapped(x):
    return pltpu.roll(x, RANK, 1)


def order_matrix(transposed):
    row = lax.broadcasted_iota(jnp.int32, (128, 128), 1 if transposed else 0)
    col = lax.broadcasted_iota(jnp.int32, (128, 128), 0 if transposed else 1)
    at = col % RANK
    source = jnp.where(at < 32, 2 * at, 2 * at - 63) + (col // RANK) * RANK
    return jnp.where(row == source, 1.0, 0.0).astype(BF)


def unpack_rows(load, tiles, block):
    for i in range(ROWS):
        x = load(i).astype(F32)
        tiles[0, pl.ds(i * PITCH, 8), :] = x[:8]
        tiles[1, pl.ds(i * PITCH, 8), :] = x[8:]
    for s in range(16):
        block(s, tiles[s // 8, pl.ds(s % 8, ROWS, stride=PITCH), :])


def pack_transfer(load, tiles, order, write):
    held = [None] * 16

    def keep(s, x):
        held[s] = x.astype(BF)

    unpack_rows(load, tiles, keep)
    ordered = dot(jnp.concatenate(held, axis=0), order)
    for s in range(16):
        x = ordered[s * ROWS : (s + 1) * ROWS]
        y = swapped(x)
        parent_odd = (s // 2) % 2
        rows = [y, x] if parent_odd else [x, y]
        write(s // 2, s % 2, jnp.concatenate(rows, axis=0).astype(BF))


def pack_kernel(transfer, ee, tiles):
    order = order_matrix(False)

    def groups(i, _):
        for u in range(2):
            g = 2 * i + u
            base = pl.multiple_of(g * 16, 16)

            def write(m, child, value, g=g):
                ee[g * 8 + m, pl.ds(child * RANK, RANK), :] = value

            pack_transfer(
                lambda i, base=base: transfer[pl.ds(base, 16), pl.ds(i * 128, 128)],
                tiles.at[u],
                order,
                write,
            )
        return 0

    lax.fori_loop(0, transfer.shape[0] // 32, groups, 0)


def blocks_kernel(coupling, blocks, tiles):
    for k in range(FAR):

        def groups(i, _):
            for u in range(2):
                g = 2 * i + u
                base = pl.multiple_of(g * 16, 16)

                def write(s, c, g=g):
                    y = swapped(c)
                    rows = [y, c] if s % 2 else [c, y]
                    blocks[g * 16 + s, k * RANK : (k + 1) * RANK, :] = jnp.concatenate(
                        rows, axis=0
                    ).astype(BF)

                unpack_rows(
                    lambda i, base=base: coupling[k, pl.ds(base, 16), pl.ds(i * 128, 128)],
                    tiles.at[u],
                    write,
                )
            return 0

        lax.fori_loop(0, 2 * LEAF_DEV // 32, groups, 0)


def pair_list(lists, counts, first):
    shape = lists.shape
    partner = lists - first
    live = lax.broadcasted_iota(jnp.int32, shape, 0) < counts
    local = live & (partner >= LEAF_DEV) & (partner < 2 * LEAF_DEV)
    before = lax.broadcasted_iota(jnp.int32, (LEAF_DEV, LEAF_DEV), 0)
    before = before < lax.broadcasted_iota(jnp.int32, (LEAF_DEV, LEAF_DEV), 1)
    above = lax.broadcasted_iota(jnp.int32, (NEAR, NEAR), 1)
    above = above < lax.broadcasted_iota(jnp.int32, (NEAR, NEAR), 0)

    def ranks(mask):
        flag = jnp.where(mask, 1.0, 0.0)
        line = jnp.broadcast_to(jnp.sum(flag, axis=1, keepdims=True), shape)
        rank = dot(flag.astype(BF), jnp.where(before, 1.0, 0.0).astype(BF))
        rank += dot(jnp.where(above, 1.0, 0.0).astype(BF), line.astype(BF))
        return rank, jnp.sum(jnp.sum(flag, axis=1, keepdims=True), axis=0, keepdims=True)

    rank_local, n_local = ranks(local)
    rank_other, n_other = ranks(live & ~local)
    rank = jnp.where(local, rank_local, jnp.where(live, rank_other + n_local, -1.0))
    rank = jnp.concatenate([rank, jnp.zeros((NEAR, 128 - LEAF_DEV), F32)], axis=1).T
    slot = lax.broadcasted_iota(jnp.int32, (LEAF_DEV, PAIRS), 1).astype(F32)
    row = lax.broadcasted_iota(jnp.int32, shape, 0)
    leaf = lax.broadcasted_iota(jnp.int32, shape, 1).astype(F32)
    known = jnp.where(live, partner, 0).astype(F32)
    found = jnp.zeros((NEAR, PAIRS), F32)
    for m in range(NEAR):
        hit = jnp.where(rank[:LEAF_DEV, m : m + 1] == slot, 1.0, 0.0).astype(BF)
        what = jnp.where(row == 0, known[m : m + 1], jnp.where(row == 1, leaf, 1.0))
        found += dot(what.astype(BF), hit)
    code = jnp.where(found[2:3] > 0.5, found[0:1] * LEAF_DEV + found[1:2], 3.0 * LEAF_DEV**2)
    at = lax.broadcasted_iota(jnp.int32, code.shape, 1)
    code = jnp.where(at == PAIRS - 2, n_local, code)
    return jnp.where(at == PAIRS - 1, n_local + n_other, code).astype(jnp.int32)


def up_kernel(
    where,
    lists_in,
    counts_in,
    vec_in,
    coords_in,
    basis_in,
    transfer_in,
    sk,
    dev,
    ee,
    xs,
    wide,
    pairs,
    lists,
    counts,
    coords,
    basis,
    transfer,
    tiles,
    nat,
    sem,
):
    copies = [
        pltpu.make_async_copy(transfer_in, transfer, sem.at[0]),
        pltpu.make_async_copy(vec_in, wide.at[pl.ds(0, VECS)], sem.at[1]),
        pltpu.make_async_copy(basis_in, basis, sem.at[2]),
        pltpu.make_async_copy(coords_in, coords, sem.at[3]),
        pltpu.make_async_copy(lists_in, lists, sem.at[4]),
        pltpu.make_async_copy(counts_in, counts, sem.at[5]),
    ]
    for c in copies:
        c.start()
    order = order_matrix(False)
    copies[0].wait()

    def group(g, _):
        base = pl.multiple_of(g * 16, 16)

        def write(m, child, value):
            ee[g * 8 + m, pl.ds(child * RANK, RANK), :] = value

        pack_transfer(
            lambda i: transfer[pl.ds(base, 16), pl.ds(i * 128, 128)], tiles, order, write
        )
        return 0

    lax.fori_loop(0, 4, group, 0)
    copies[1].wait()
    for c in copies[3:]:
        c.wait()
    pairs[...] = pair_list(lists[...], counts[...], (where[0] - 1) * LEAF_DEV)
    for i in range(LEAF_DEV):
        lanes = slice(i * LEAF, (i + 1) * LEAF)
        xs[i] = pieces(wide[0:VECS, lanes])
        c = coords[:, lanes]
        blank = jnp.zeros((1, LEAF), F32)
        wide[VECS : VECS + 8, lanes] = jnp.concatenate([c, blank, c, blank], axis=0)
    copies[2].wait()
    for m in range(LEAF_DEV // 2):
        x = xs[2 * m : 2 * m + 2].reshape(64, LEAF)
        b = basis[2 * m : 2 * m + 2].reshape(128, LEAF)
        r = dot(x, b, NT)
        nat[m] = joined(folded(r[:32]), folded(r[32:]))
    for m in range(LEAF_DEV // 2):
        sk[16 + m] = folded(dot(pieces(nat[m]), order))
    half = LEAF_DEV // 2
    while half > 1:
        for m in range(half, 2 * half, 2):
            a = folded(dot(pieces(sk[m]), ee[m]))
            b = folded(dot(pieces(sk[m + 1]), ee[m + 1]))
            sk[m // 2] = joined(a, b)
        half = half // 2
    top = folded(dot(pieces(sk[1]), ee[1]))
    sk[0] = jnp.where(low_lanes(top.shape), 0.0, top)
    dev[...] = jnp.broadcast_to(joined(swapped(top[:8]), top[8:])[None], dev.shape)
    for m in range(LEAF_DEV):
        for h in range(2):
            lanes = slice((2 * m + h) * 128, (2 * m + h + 1) * 128)
            wide[24:32, lanes] = sk[m, 8 * h : 8 * h + 8]


def split3(v):
    h1 = v.astype(BF).astype(F32)
    h2 = (v - h1).astype(BF).astype(F32)
    return h1, h2, (v - h1 - h2).astype(BF).astype(F32)


def features(c):
    row = lax.broadcasted_iota(jnp.int32, c.shape, 0)
    low = row < 4
    s = jnp.where(row % 4 < 3, (c - 0.5) * SIGMA, 0.0)
    h1, h2, h3 = split3(s)
    size = jnp.sum(jnp.where(low, s * s, 0.0), axis=0, keepdims=True)
    n1, n2, n3 = split3(size)
    j1, j2, j3 = split3(size + JITTER_SQ * SIGMA * SIGMA)

    def rows(*values):
        x = jnp.zeros(c.shape, F32)
        for at, v in enumerate(values):
            x = jnp.where(row == at, v, x)
        return x

    cross = -2.0 * jnp.where(low, h1, h2)
    own = [cross, cross, -2.0 * jnp.where(low, h3, h1), rows(j1, j2, j3, 1.0, 1.0, 1.0)]
    partner = [h1, h2, jnp.where(low, h1, h3), rows(1.0, 1.0, 1.0, n1, n2, n3)]
    return jnp.concatenate(own, axis=0), jnp.concatenate(partner, axis=0)


def four_leaves(c):
    own, partner = features(c)
    parts = [partner[:, q * LEAF : (q + 1) * LEAF] for q in range(4)]
    return own.astype(BF), jnp.concatenate(parts, axis=0).T.astype(BF)


def own_kernel(wide, partner, own):
    def prepare(i, _):
        lanes = pl.ds(pl.multiple_of(i * 4 * LEAF, 4 * LEAF), 4 * LEAF)
        mine, partner[i] = four_leaves(wide[VECS : VECS + 8, lanes])
        for q in range(4):
            own[4 * i + q, 0:96] = jnp.zeros((96, LEAF), BF)
            own[4 * i + q, 96:128] = mine[:, q * LEAF : (q + 1) * LEAF]
            own[4 * i + q, 128:224] = jnp.zeros((96, LEAF), BF)
        return 0

    lax.fori_loop(0, LEAF_DEV // 4, prepare, 0)


def other_kernel(xs_own, partner_own, before, after, xs, partner):
    xs[pl.ds(LEAF_DEV, LEAF_DEV)] = xs_own[...]
    xs[3 * LEAF_DEV] = jnp.zeros((32, LEAF), BF)
    partner[pl.ds(LEAF_DEV // 4, LEAF_DEV // 4)] = partner_own[...]
    partner[3 * LEAF_DEV // 4] = partner_own[0]

    def prepare(i, _):
        for at, wide in ((0, before), (2, after)):
            for q in range(4):
                lanes = pl.ds(pl.multiple_of((4 * i + q) * LEAF, LEAF), LEAF)
                xs[at * LEAF_DEV + 4 * i + q] = pieces(wide[0:VECS, lanes])
            lanes = pl.ds(pl.multiple_of(i * 4 * LEAF, 4 * LEAF), 4 * LEAF)
            _, partner[at * LEAF_DEV // 4 + i] = four_leaves(wide[VECS : VECS + 8, lanes])
        return 0

    lax.fori_loop(0, LEAF_DEV // 4, prepare, 0, unroll=2)


def near_kernel(chunk, pairs, xs, partner, own, *rest):
    out = rest[-1]
    start = lax.div(pairs[0, PAIRS - 2], GROUP)
    if chunk == 0:
        out[...] = jnp.zeros_like(out)
        begin, end, skip = 0, start, LEAF_DEV
    else:
        out[...] = rest[0][...]
        begin, end, skip = start, lax.div(pairs[0, PAIRS - 1] + GROUP - 1, GROUP), 0

    def step(i, _):
        for g in range(GROUP):
            code = pairs[0, i * GROUP + g]
            p = (code >> 5) - skip
            c = code & (LEAF_DEV - 1)
            rows = pl.ds(pl.multiple_of(96 - (p & 3) * 32, 32), 128)
            t = dot(partner[p >> 2], own[c, rows, :])
            u = t * lax.rsqrt(t)
            k = (u + LOG2E) * jnp.exp2(-u)
            khi = k.astype(BF)
            klo = (k - khi.astype(F32)).astype(BF)
            x = xs[p]
            r = folded(dot(x, khi)) + dot(x[:VECS], klo)
            lanes = pl.ds(pl.multiple_of(c * LEAF, LEAF), LEAF)
            out[:, lanes] = out[:, lanes] + r
        return 0

    lax.fori_loop(begin, end, step, 0)


def top_kernel(lists, where, tiles_in, ee, coupling, out, q, blocks, raw, sem):
    d = where[0]
    devices = DEVICES
    levels = devices.bit_length() - 1
    order = order_matrix(False)
    nodes = [(devices + d) >> (levels - level) for level in range(levels + 1)]
    copies = [
        pltpu.make_async_copy(coupling.at[nodes[level]], raw.at[level], sem.at[level])
        for level in range(1, levels + 1)
    ]
    for c in copies:
        c.start()

    def place(m, _):
        a = tiles_in[2 * m]
        b = tiles_in[2 * m + 1]
        q[devices // 2 + m, 0:8] = joined(a, swapped(b))
        q[devices // 2 + m, 8:16] = joined(swapped(a), b)
        return 0

    lax.fori_loop(0, devices // 2, place, 0, unroll=8)

    half = devices // 2

    def parents(m):
        a = folded(dot(pieces(q[m]), ee[m]))
        b = folded(dot(pieces(q[m + 1]), ee[m + 1]))
        return joined(a, b)

    while half >= 2:
        if half >= 64:

            def some(i, _, half=half):
                for u in range(16):
                    m = half + 32 * i + 2 * u
                    q[m // 2] = parents(m)
                return 0

            lax.fori_loop(0, half // 32, some, 0)
        else:
            for m in range(half, 2 * half, 2):
                q[m // 2] = parents(m)
        half = half // 2
    for c in copies:
        c.wait()
    own = []
    for level in range(1, levels + 1):
        a = nodes[level]
        x = raw[level].astype(F32)
        for i in range(ROWS):
            blocks[pl.ds(i * 8, 2), :] = x[:, i * 128 : (i + 1) * 128]
        rhs, lhs = [], []
        for k in range(2):
            c = blocks[pl.ds(k, ROWS, stride=8), :]
            rhs += [c, swapped(c)]
            slot = lists[k, a]
            v = q[slot // 2]
            lhs.append(jnp.where(slot % 2 == k, v, swapped(v)))
        r = dot(pieces(joined(*lhs)), jnp.concatenate(rhs, axis=0).astype(BF))
        r = folded(dot(pieces(folded(r)), order))
        odd = a % 2 == 1
        r = jnp.where(odd, swapped(r), r)
        own.append(jnp.where(low_lanes(r.shape) != odd, r, 0.0))
    path = own[0]
    for level in range(2, levels + 1):
        r = folded(dot(pieces(path), ee[nodes[level - 1]], NT))
        odd = nodes[level] % 2 == 1
        path = jnp.where(low_lanes(r.shape) != odd, r, 0.0) + own[level - 1]
    out[...] = jnp.where(nodes[levels] % 2 == 1, path, swapped(path))


def down_kernel(
    lists, where, sk_own, before, after, blocks, ee, basis, path, near, out, table, nat, field
):
    slots = 2 * LEAF_DEV
    first = (where[0] - 1) * slots
    order = order_matrix(False)
    back = order_matrix(True)

    def double(m, _):
        lanes = pl.ds(pl.multiple_of(m * 256, 256), 256)
        for at, wide in enumerate((before, None, after)):
            if wide is None:
                x = sk_own[m]
            else:
                x = wide[24:32, lanes]
                x = jnp.concatenate([x[:, :128], x[:, 128:]], axis=0)
            y = swapped(x)
            table[at * slots + 2 * m] = pieces(joined(x, y))
            table[at * slots + 2 * m + 1] = pieces(joined(y, x))
        return 0

    lax.fori_loop(0, LEAF_DEV, double, 0, unroll=2)

    def couple(i, _):
        for u in range(8):
            m = jnp.maximum(8 * i + u, 1)
            sides = []
            for side in range(2):
                j = 2 * m + side
                parts = []
                for k in range(0, FAR, 2):
                    a = table[lists[k, j] - first]
                    b = table[lists[k + 1, j] - first]
                    parts.append(joined(a, b))
                sides.append(folded(dot(jnp.concatenate(parts, axis=1), blocks[j])))
            nat[m] = joined(*sides)
        return 0

    nat[0] = jnp.zeros((VECS, 128), F32)
    lax.fori_loop(0, LEAF_DEV // 8, couple, 0)
    for i in range(LEAF_DEV // 8):
        x = nat[8 * i : 8 * i + 8].reshape(8 * VECS, 128)
        x = folded(dot(pieces(x), order))
        field[8 * i : 8 * i + 8] = x.reshape(8, VECS, 128)
    field[0] = path[...]
    for m in range(1, LEAF_DEV):
        x = field[m // 2]
        x = jnp.where(low_lanes(x.shape) != (m % 2 == 1), x, 0.0)
        field[m] = field[m] + folded(dot(pieces(x), ee[m], NT))
    for m in range(LEAF_DEV // 2):
        x = folded(dot(pieces(field[LEAF_DEV // 2 + m]), back))
        low = low_lanes(x.shape)
        lhs = jnp.concatenate(
            [pieces(jnp.where(low, x, 0.0)), pieces(jnp.where(low, 0.0, x))], axis=0
        )
        r = dot(lhs, basis[2 * m : 2 * m + 2].reshape(128, LEAF))
        for side in range(2):
            lanes = slice((2 * m + side) * LEAF, (2 * m + side + 1) * LEAF)
            far = folded(r[32 * side : 32 * side + 32])
            out[:, lanes] = far + near[:, lanes] * (LN2 / math.sqrt(LEAF))


def call(kernel, out_shape, in_specs, scratch=(), name=None, us=1, mib=16):
    return pl.pallas_call(
        kernel,
        out_shape=out_shape,
        in_specs=in_specs,
        out_specs=jax.tree.map(lambda _: VMEM, out_shape),
        scratch_shapes=list(scratch),
        compiler_params=pltpu.CompilerParams(vmem_limit_bytes=mib << 20),
        name=name,
        cost_estimate=pl.CostEstimate(
            flops=us * 10**9, bytes_accessed=us * 10**6, transcendentals=0
        ),
    )


def shaped(shape, dtype=F32):
    return jax.ShapeDtypeStruct(shape, dtype)


def per_device(
    vectors,
    coords,
    leaf_basis,
    transfer,
    coupling,
    near_list,
    near_count,
    local_list,
    top_transfer,
    top_coupling,
    top_list,
):
    devices = lax.axis_size(AXES)
    position = lax.axis_index(AXES).astype(jnp.int32)
    where = position.reshape(1)
    up = [(i, i + 1) for i in range(devices - 1)]
    down = [(j, i) for i, j in up]
    sk, dev, ee, xs_own, wide, pairs = call(
        up_kernel,
        (
            shaped((LEAF_DEV, VECS, 128)),
            shaped((DEVICES, 8, 128)),
            shaped((LEAF_DEV, 128, 128), BF),
            shaped((LEAF_DEV, 32, LEAF), BF),
            shaped((32, LEAF_DEV * LEAF)),
            shaped((1, PAIRS), jnp.int32),
        ),
        [SMEM] + [HBM] * 6,
        [
            pltpu.VMEM((NEAR, LEAF_DEV), jnp.int32),
            pltpu.VMEM((1, LEAF_DEV), jnp.int32),
            pltpu.VMEM((3, LEAF_DEV * LEAF), F32),
            pltpu.VMEM((LEAF_DEV, RANK, LEAF), BF),
            pltpu.VMEM((2 * LEAF_DEV, RANK * RANK), BF),
            pltpu.VMEM((2, PITCH * ROWS, 128), F32),
            pltpu.VMEM((16, VECS, 128), F32),
            pltpu.SemaphoreType.DMA((6,)),
        ],
        "up",
    )(
        where,
        *(
            pltpu.with_memory_space_constraint(x, pltpu.HBM)
            for x in (
                near_list.T,
                near_count.reshape(1, LEAF_DEV),
                vectors,
                coords,
                leaf_basis,
                transfer,
            )
        ),
    )
    order_scratch = [pltpu.VMEM((2, 2, PITCH * ROWS, 128), F32)]
    tied = lax.optimization_barrier
    tiles = lax.all_to_all(dev, AXES, 0, 0, tiled=True)
    before = lax.ppermute(wide, AXES, up)
    after = lax.ppermute(wide, AXES, down)
    partner_own, own = call(
        own_kernel,
        (
            shaped((LEAF_DEV // 4, LEAF, 128), BF),
            shaped((LEAF_DEV, 224, LEAF), BF),
        ),
        [VMEM],
        (),
        "own",
        us=2,
    )(wide)
    near = call(
        functools.partial(near_kernel, 0),
        shaped((VECS, LEAF_DEV * LEAF)),
        [SMEM] + [VMEM] * 3,
        (),
        "near0",
        us=8,
    )(pairs, xs_own, partner_own, own)
    near, before, after = tied((near, before, after))
    xs, partner = call(
        other_kernel,
        (
            shaped((3 * LEAF_DEV + 1, 32, LEAF), BF),
            shaped((3 * LEAF_DEV // 4 + 1, LEAF, 128), BF),
        ),
        [VMEM] * 4,
        (),
        "other",
        us=2,
    )(xs_own, partner_own, before, after)
    near = call(
        functools.partial(near_kernel, 1),
        shaped((VECS, LEAF_DEV * LEAF)),
        [SMEM] + [VMEM] * 4,
        (),
        "near1",
        us=8,
    )(pairs, xs, partner, own, near)
    tiles, near = tied((tiles, near))
    upper, stored, _ = tied((top_transfer, coupling, tiles))
    ee_top = call(
        pack_kernel, shaped((devices, 128, 128), BF), [VMEM], order_scratch, "pack", us=4
    )(upper)
    levels = devices.bit_length() - 1
    path = call(
        top_kernel,
        shaped((VECS, 128)),
        [SMEM] * 2 + [VMEM] * 2 + [HBM],
        [
            pltpu.VMEM((devices, VECS, 128), F32),
            pltpu.VMEM((256, 128), F32),
            pltpu.VMEM((levels + 1, 2, RANK * RANK), BF),
            pltpu.SemaphoreType.DMA((levels + 1,)),
        ],
        "top",
        us=6,
    )(
        top_list.T,
        where,
        tiles,
        ee_top,
        pltpu.with_memory_space_constraint(top_coupling, pltpu.HBM),
    )
    blocks = call(
        blocks_kernel,
        shaped((2 * LEAF_DEV, FAR * RANK, 128), BF),
        [VMEM],
        order_scratch,
        "blocks",
        us=3,
    )(jnp.transpose(stored, (1, 0, 2)))
    return call(
        down_kernel,
        shaped((VECS, LEAF_DEV * LEAF)),
        [SMEM] * 2 + [VMEM] * 8,
        [
            pltpu.VMEM((6 * LEAF_DEV, 32, 128), BF),
            pltpu.VMEM((LEAF_DEV, VECS, 128), F32),
            pltpu.VMEM((LEAF_DEV, VECS, 128), F32),
        ],
        "down",
    )(local_list.T, where, sk, before, after, blocks, ee, leaf_basis, path, near)


def solution(mesh):
    split = P(None, AXES)
    return jax.shard_map(
        per_device,
        mesh=mesh,
        in_specs=(
            split,
            split,
            P(AXES, None, None),
            P(AXES, None),
            P(AXES, None, None),
            P(AXES, None),
            P(AXES),
            P(AXES, None),
            P(),
            P(),
            P(),
        ),
        out_specs=split,
        check_vma=False,
    )
```
